32 devices in a mesh: sub: 8 (over y, x, core), grp: 4 (over z).
Axes of the slice: x: 2, y: 2, z: 4, core: 2. Of those that a mesh axis runs over, the one named last changes fastest.
Arguments:
- res_inner: bfloat16 [2048, 16, 144], P(('sub', 'grp')), may hold values from -6 to 6
- res_face: bfloat16 [1024, 16, 144], P(('sub', 'grp')), may hold values from -6 to 6
- inner_inv: bfloat16 [2048, 144, 144], P(('sub', 'grp')), may hold values from -0.5 to 0.5
- face_coupling: bfloat16 [1024, 144, 144], P(('sub', 'grp')), may hold values from -0.5 to 0.5
- face_elem: int32 [32, 32], P(('sub', 'grp')), may hold values from 0 to 63
- face_inv: bfloat16 [1024, 144, 144], P(('sub', 'grp')), may hold values from -0.5 to 0.5
- coarse_basis: bfloat16 [1024, 64, 144], P(('sub', 'grp')), may hold values from -0.0625 to 0.0625
- coarse_map: int32 [32, 64], P(('sub', 'grp')), may hold values from 0 to 511
- coarse_inv: float32 [512, 512], P('grp'), as said below
- recv_index: int32 [32, 32], P(('sub', 'grp')), may hold values from 0 to 8, as said below
- sharers: int32 [32, 32], P(('sub', 'grp')), may hold values from 0 to 32, as said below
Outputs:
- inner_out: bfloat16 [2048, 16, 144], P(('sub', 'grp'))
- face_out: bfloat16 [1024, 16, 144], P(('sub', 'grp'))
The draws below stay inside these ranges and needn't reach their ends.
Inputs may be any that keep to these rules, and one draw needn't show every extreme that they name: `recv_index`: row o gives, for each subdomain s at position s, the index among the 8 blocks owned by subdomain o that slot o of subdomain s refers to, or 8 where that slot is unused. `sharers`: for a used slot, the number of used slots of all subdomains that refer to the same owned block, up to all 32 of them, which some block reaches; 0 exactly for unused slots. coarse_inv is symmetric.
All inputs are finite; a program needn't handle non-finite values.
Results may differ from the reference program's by a relative error of at most 0.006.
Values may be sent and summed in bfloat16 or wider, within the bound.
No kernel may reach another device: no remote copies, remote signals or barrier semaphores. Data moves between devices by JAX's collectives and lax.ppermute only.
A program may use at most 128 MiB of HBM per device.

```python
import math
import jax
import jax.numpy as jnp
from jax import lax

B = 144
R = 16
E = 64
NC = 64
SUBS = 32
FACES = 32
OWNED = 8
NCG = 512


def interface_tables(key):
    base = jax.random.fold_in(key, 5)
    key_load, key_roll, key_pick = jax.random.split(base, 3)
    count = SUBS
    load = jax.random.randint(key_load, (count,), 1, 5)
    roll = jax.random.randint(key_roll, (count, count), 0, 4)
    source = jnp.arange(count, dtype=jnp.int32)[:, None]
    target = jnp.arange(count, dtype=jnp.int32)[None, :]
    neighbour = target == (source + 1) % count
    live = roll < load[None, :]
    live = jnp.logical_or(live, target == 0)
    live = jnp.logical_or(live, neighbour)
    live = jnp.logical_or(live, target == source)
    picks = jax.random.randint(key_pick, (count, count), 0, OWNED)
    picks = jnp.where(jnp.logical_or(target == source, target == 0), 0, picks)
    index = jnp.where(live, picks, OWNED).astype(jnp.int32)
    owner_view = index.T
    levels = jnp.arange(OWNED + 1, dtype=jnp.int32)
    hits = jnp.sum((owner_view[:, :, None] == levels[None, None, :]).astype(jnp.int32), axis=1)
    owner_rows = jnp.broadcast_to(target, (count, count))
    shared = jnp.where(live, hits[owner_rows, index], 0).astype(jnp.int32)
    return (owner_view, shared)


def draw_recv_index(key, part):
    owner_view, shared = interface_tables(key)
    return owner_view


def draw_sharers(key, part):
    owner_view, shared = interface_tables(key)
    return shared


def draw_coarse_inv(key, part):
    base = jax.random.fold_in(key, 11)
    key_raw, key_diag = jax.random.split(base, 2)
    count = NCG
    raw = jax.random.normal(key_raw, (count, count), jnp.float32)
    symmetric = (raw + raw.T) * (0.35 / math.sqrt(count))
    diagonal = jnp.exp(jax.random.uniform(key_diag, (count,), jnp.float32, 0.0, 1.1))
    identity = jnp.eye(count, dtype=jnp.float32)
    full = symmetric + identity * diagonal[None, :]
    return full.astype(jnp.float32)


def set_ends(drawn, rng, smallest, high):
    shape = drawn.shape
    place = [jax.random.randint(jax.random.fold_in(rng, axis), (), 0, shape[axis]) for axis in range(len(shape))]
    drawn = drawn.at[tuple(place)].set(smallest)
    longest = shape.index(max(shape))
    place[longest] = (place[longest] + 1) % shape[longest]
    return drawn.at[tuple(place)].set(high)


def steps_of(rng, extent, shards, least, largest):
    def one(axis_at, blocks):
        draws = jax.random.uniform(jax.random.fold_in(jax.random.fold_in(rng, 6), axis_at), (blocks,), jnp.float32, least / len(shards), largest / len(shards))
        return jnp.repeat(jnp.exp(draws), extent[axis_at] // blocks).reshape((-1,) + (1,) * (len(extent) - axis_at - 1))

    loudness = one(*shards[0])
    for cut in shards[1:]:
        loudness = loudness * one(*cut)
    return loudness


def normal_values(own_key, shape, spread, bound, shards=(), kind=jnp.bfloat16):
    values = spread * jax.random.normal(own_key, shape, jnp.float32)
    if shards:
        values = values * steps_of(own_key, shape, shards, -0.22, 0.18)
    return jnp.clip(values, -bound, bound).astype(kind)


def setup_inputs(seed: int = 0) -> dict:
    key_of = jax.random.split(jax.random.key(seed), 12)
    return {
        "res_inner": normal_values(key_of[0], (SUBS * E, R, B), 1.0, 6.0, ((0, 32),)),
        "res_face": normal_values(key_of[1], (SUBS * FACES, R, B), 1.0, 6.0, ((0, 32),)),
        "inner_inv": normal_values(key_of[2], (SUBS * E, B, B), B ** -0.5, 0.5, ((0, 32),)),
        "face_coupling": normal_values(key_of[3], (SUBS * FACES, B, B), B ** -0.5, 0.5, ((0, 32),)),
        "face_elem": set_ends(jax.random.randint(key_of[4], (SUBS, FACES), 0, E), jax.random.fold_in(key_of[4], 1), 0, E - 1).astype(jnp.int32),
        "face_inv": normal_values(key_of[5], (SUBS * FACES, B, B), B ** -0.5, 0.5, ((0, 32),)),
        "coarse_basis": normal_values(key_of[6], (SUBS * FACES, NC, B), (B * NC) ** -0.5, 0.0625, ((0, 32),)),
        "coarse_map": set_ends(jax.random.randint(key_of[7], (SUBS, NC), 0, NCG), jax.random.fold_in(key_of[7], 1), 0, NCG - 1).astype(jnp.int32),
        "coarse_inv": draw_coarse_inv(jax.random.fold_in(key_of[11], 71), 0),
        "recv_index": draw_recv_index(jax.random.fold_in(key_of[11], 71), 0),
        "sharers": draw_sharers(jax.random.fold_in(key_of[11], 71), 0),
    }


def assemble(sent, recv_index):
    columns = jnp.swapaxes(sent, 0, 1)

    def per_owner(items):
        column, index = items
        summed = jax.ops.segment_sum(column.astype(jnp.float32), index, num_segments=OWNED + 1)[:OWNED].astype(jnp.bfloat16)
        padded = jnp.concatenate([summed, jnp.zeros((1,) + summed.shape[1:], jnp.bfloat16)], 0)
        return padded[index]

    returned = lax.map(per_owner, (columns, recv_index))
    return jnp.swapaxes(returned, 0, 1)


def reference(res_inner, res_face, inner_inv, face_coupling, face_elem, face_inv, coarse_basis, coarse_map, coarse_inv, recv_index, sharers):
    inner = res_inner.reshape(SUBS, E, R, B)
    faced = res_face.reshape(SUBS, FACES, R, B)
    inverse = inner_inv.reshape(SUBS, E, B, B)
    coupling = face_coupling.reshape(SUBS, FACES, B, B)
    local_inv = face_inv.reshape(SUBS, FACES, B, B)
    basis = coarse_basis.reshape(SUBS, FACES, NC, B)
    weights = jnp.where(sharers > 0, 1.0 / jnp.maximum(sharers, 1).astype(jnp.float32), 0.0).astype(jnp.float32)

    def condense(items):
        block, face, inv_block, couple, elems, weight = items
        inner_w = jnp.einsum('erb,ecb->erc', block.astype(jnp.float32), inv_block.astype(jnp.float32)).astype(jnp.bfloat16)
        nearby = inner_w[elems]
        condensed = face.astype(jnp.float32) - jnp.einsum('lrb,lcb->lrc', nearby.astype(jnp.float32), couple.astype(jnp.float32))
        return (weight[:, None, None] * condensed).astype(jnp.bfloat16)

    sent = lax.map(condense, (inner, faced, inverse, coupling, face_elem, weights))
    gathered = assemble(sent, recv_index)
    restricted = (weights[:, :, None, None] * gathered.astype(jnp.float32)).astype(jnp.bfloat16)

    def project(items):
        base, restr = items
        return jnp.einsum('ljb,lrb->jr', base.astype(jnp.float32), restr.astype(jnp.float32))

    local_coarse = lax.map(project, (basis, restricted))
    coarse_rhs = jax.ops.segment_sum(local_coarse.reshape(SUBS * NC, R), coarse_map.reshape(-1), num_segments=NCG)
    coarse_sol = jnp.dot(coarse_inv, coarse_rhs, precision=lax.Precision.HIGHEST)
    picked = coarse_sol[coarse_map].astype(jnp.bfloat16)

    def correct(items):
        base, pick, restr, inv_block, weight = items
        coarse_part = jnp.einsum('ljb,jr->lrb', base.astype(jnp.float32), pick.astype(jnp.float32))
        local_part = jnp.einsum('lrb,lcb->lrc', restr.astype(jnp.float32), inv_block.astype(jnp.float32))
        return (weight[:, None, None] * (coarse_part + local_part)).astype(jnp.bfloat16)

    weighted = lax.map(correct, (basis, picked, restricted, local_inv, weights))
    face_out = assemble(weighted, recv_index)

    def extend(items):
        block, face_val, couple, elems, inv_block = items
        contrib = jnp.einsum('lrc,lcb->lrb', face_val.astype(jnp.float32), couple.astype(jnp.float32))
        scattered = jax.ops.segment_sum(contrib, elems, num_segments=E)
        inner_rhs = (block.astype(jnp.float32) - scattered).astype(jnp.bfloat16)
        return jnp.einsum('erb,ecb->erc', inner_rhs.astype(jnp.float32), inv_block.astype(jnp.float32)).astype(jnp.bfloat16)

    inner_out = lax.map(extend, (inner, face_out, coupling, face_elem, inverse))
    return inner_out.reshape(SUBS * E, R, B), face_out.reshape(SUBS * FACES, R, B)
```

```python
import jax
import jax.numpy as jnp
from jax import lax
from jax.sharding import PartitionSpec as P

AXES = ("sub", "grp")
DIGIT = 128


def exchange(blocks, axes=AXES):
    return lax.all_to_all(blocks, axes, split_axis=0, concat_axis=0, tiled=True)


def body(
    res_inner,
    res_face,
    inner_inv,
    face_coupling,
    face_elem,
    face_inv,
    coarse_basis,
    coarse_map,
    coarse_inv,
    recv_index,
    sharers,
):
    num_faces, rhs, width = res_face.shape
    num_owned = num_faces // 4
    elements = res_inner.shape[0]
    row_count, num_coarse = coarse_inv.shape
    groups = num_coarse // row_count
    local = coarse_map.shape[1]
    counts = sharers[0]
    weights = jnp.where(counts > 0, 1.0 / jnp.maximum(counts, 1).astype(jnp.float32), 0.0)
    owner_onehot = (
        recv_index[0][None, :] == jnp.arange(num_owned, dtype=jnp.int32)[:, None]
    ).astype(jnp.bfloat16)

    def owner_assemble(received):
        flattened = received.reshape(num_faces, -1)
        owner_sum = jnp.dot(owner_onehot, flattened, preferred_element_type=jnp.float32).astype(
            jnp.bfloat16
        )
        return jnp.einsum(
            "of,ok->fk", owner_onehot, owner_sum, preferred_element_type=jnp.float32
        ).astype(jnp.bfloat16).reshape(num_faces, rhs, width)

    inner_w = jnp.einsum(
        "erb,ecb->erc", res_inner, inner_inv, preferred_element_type=jnp.float32
    ).astype(jnp.bfloat16)
    nearby = inner_w[face_elem[0]]
    condensed = res_face.astype(jnp.float32) - jnp.einsum(
        "lrb,lcb->lrc", nearby, face_coupling, preferred_element_type=jnp.float32
    )
    sent = (weights[:, None, None] * condensed).astype(jnp.bfloat16)
    digits = jnp.stack([coarse_map[0] // DIGIT, coarse_map[0] % DIGIT]).astype(jnp.bfloat16)
    digits = jnp.pad(digits, ((0, rhs - 2), (0, 0)))
    digits = jnp.broadcast_to(digits[None], (num_faces,) + digits.shape)
    first = exchange(jnp.concatenate([sent, digits], -1))
    maps = first[:, :2, width:].astype(jnp.int32)
    maps = (maps[:, 0] * DIGIT + maps[:, 1]).reshape(-1)
    gathered = exchange(owner_assemble(first[:, :, :width]))
    restricted = (weights[:, None, None] * gathered.astype(jnp.float32)).astype(jnp.bfloat16)
    local_coarse = jnp.einsum(
        "ljb,lrb->jr", coarse_basis, restricted, preferred_element_type=jnp.float32
    )
    packed = local_coarse.reshape(-1, 128)
    all_coarse = exchange(jnp.broadcast_to(packed[None], (num_faces,) + packed.shape))
    all_coarse = all_coarse.reshape(num_faces * local, rhs)
    every = (maps[None, :] == jnp.arange(num_coarse, dtype=jnp.int32)[:, None]).astype(jnp.float32)
    coarse_rhs = jnp.dot(every, all_coarse, precision=lax.Precision.HIGHEST)
    row_part = jnp.dot(coarse_inv, coarse_rhs, precision=lax.Precision.HIGHEST)
    packed = row_part.reshape(-1, 128)
    coarse_sol = exchange(jnp.broadcast_to(packed[None], (groups,) + packed.shape), "grp")
    coarse_sol = coarse_sol.reshape(num_coarse, rhs)
    coarse_onehot = (
        coarse_map[0][None, :] == jnp.arange(num_coarse, dtype=jnp.int32)[:, None]
    ).astype(jnp.float32)
    picked = jnp.einsum(
        "kj,kr->jr", coarse_onehot, coarse_sol, precision=lax.Precision.HIGHEST
    ).astype(jnp.bfloat16)
    coarse_part = jnp.einsum(
        "ljb,jr->lrb", coarse_basis, picked, preferred_element_type=jnp.float32
    )
    local_part = jnp.einsum(
        "lrb,lcb->lrc", restricted, face_inv, preferred_element_type=jnp.float32
    )
    weighted = (weights[:, None, None] * (coarse_part + local_part)).astype(jnp.bfloat16)
    face_out = exchange(owner_assemble(exchange(weighted)))
    contrib = jnp.einsum(
        "lrc,lcb->lrb", face_out, face_coupling, preferred_element_type=jnp.float32
    )
    elem_onehot = (face_elem[0][None, :] == jnp.arange(elements, dtype=jnp.int32)[:, None]).astype(
        jnp.float32
    )
    scattered = jnp.dot(
        elem_onehot, contrib.reshape(num_faces, -1), precision=lax.Precision.HIGHEST
    ).reshape(res_inner.shape)
    inner_rhs = (res_inner.astype(jnp.float32) - scattered).astype(jnp.bfloat16)
    inner_out = jnp.einsum(
        "erb,ecb->erc", inner_rhs, inner_inv, preferred_element_type=jnp.float32
    ).astype(jnp.bfloat16)
    return (inner_out, face_out)


def solution(mesh):
    block = P(AXES, None, None)
    row = P(AXES, None)
    return jax.shard_map(
        body,
        mesh=mesh,
        in_specs=(block, block, block, block, row, block, block, row, P("grp", None), row, row),
        out_specs=(block, block),
        check_vma=False,
    )
```

```python
import functools

import jax
import jax.numpy as jnp
from jax import lax
from jax.experimental import pallas as pl
from jax.experimental.pallas import tpu as pltpu
from jax.sharding import PartitionSpec as P

AXES = ("sub", "grp")
DIGIT = 128
LANES = 128
NT = (((1,), (1,)), ((), ()))
NN = (((1,), (0,)), ((), ()))
F32 = jnp.float32
BF16 = jnp.bfloat16
VMEM = pl.BlockSpec(memory_space=pltpu.VMEM)
SMEM = pl.BlockSpec(memory_space=pltpu.SMEM)
ANY = pl.BlockSpec(memory_space=pl.ANY)
GROUP = 8


def exchange(blocks):
    return lax.all_to_all(blocks, AXES, split_axis=0, concat_axis=0, tiled=True)


def dot(a, b, dims=NN):
    return lax.dot_general(a, b, dims, preferred_element_type=F32)


def omega(sharers, slot):
    count = sharers[0, slot]
    return jnp.where(count > 0, 1.0 / jnp.maximum(count, 1).astype(F32), 0.0)


def split(value):
    high = value.astype(BF16)
    return high, (value - high.astype(F32)).astype(BF16)


def pack(out, slot, value, extra):
    rhs, width = value.shape
    tail = width - LANES
    half = rhs // 2
    out[slot, 0:rhs, :] = value[:, :LANES].astype(BF16)
    end = value[:, LANES:]
    out[slot, rhs : rhs + half, :] = jnp.concatenate(
        [end[:half], end[half:], extra[:, 2 * tail :]], axis=1
    ).astype(BF16)


def unpack(ref, slot, rhs, tail):
    half = rhs // 2
    main = ref[slot, 0:rhs, :].astype(F32)
    last = ref[slot, rhs : rhs + half, :].astype(F32)
    end = jnp.concatenate([last[:, :tail], last[:, tail : 2 * tail]], axis=0)
    return jnp.concatenate([main, end], axis=1)


def loop(count, step, group=GROUP):
    group = min(group, count)

    def body(g, carry):
        for u in range(group):
            step(g * group + u)
        return carry

    lax.fori_loop(0, count // group, body, 0)


def condense_kernel(elem, sharers, cmap, inner, inv, couple, face, out, rin, invs, cps, fac, sems):
    slots, rhs, width = fac.shape
    tail = width - LANES
    chunks = slots // GROUP

    def inner_copy(l):
        return pltpu.make_async_copy(inner.at[elem[0, l]], rin.at[l], sems.at[0, l])

    def inv_copy(l):
        return pltpu.make_async_copy(inv.at[elem[0, l]], invs.at[l], sems.at[1, l])

    def couple_copy(c):
        part = pl.ds(c * GROUP, GROUP)
        return pltpu.make_async_copy(couple.at[part], cps.at[part], sems.at[2, c])

    def face_copy(c):
        part = pl.ds(c * GROUP, GROUP)
        return pltpu.make_async_copy(face.at[part], fac.at[part], sems.at[3, c])

    def start(c, carry):
        for u in range(GROUP):
            inner_copy(c * GROUP + u).start()
            inv_copy(c * GROUP + u).start()
        couple_copy(c).start()
        face_copy(c).start()
        return carry

    lax.fori_loop(0, chunks, start, 0)
    maps = cmap[...]
    digits = jnp.concatenate([maps // DIGIT, maps % DIGIT], axis=0).astype(F32)
    local = digits.shape[1]
    digits = jnp.concatenate([digits, jnp.zeros((rhs // 2 - 2, local), F32)], axis=0)
    extra = jnp.concatenate([jnp.zeros((rhs // 2, LANES - local), F32), digits], axis=1)

    def chunk(c, carry):
        for u in range(GROUP):
            inner_copy(c * GROUP + u).wait()
            inv_copy(c * GROUP + u).wait()
        couple_copy(c).wait()
        face_copy(c).wait()
        for u in range(GROUP):
            l = c * GROUP + u
            near = dot(rin[l], invs[l], NT).astype(BF16)
            value = fac[l].astype(F32) - dot(near, cps[l], NT)
            pack(out, l, omega(sharers, l) * value, extra)
        return carry

    lax.fori_loop(0, chunks, chunk, 0)


def owner_kernel(recv, got, out, sums, rounded):
    slots = got.shape[0]
    owned = sums.shape[0] - 1
    sums[...] = jnp.zeros_like(sums)

    def add(s):
        j = recv[0, s]
        sums[j] += got[s].astype(F32)

    loop(slots, add)
    rounded[...] = sums[...].astype(BF16)
    rounded[owned] = jnp.zeros(rounded.shape[1:], BF16)

    def give(s):
        out[s] = rounded[recv[0, s]]

    loop(slots, give)


def pair_maps(first, d, rhs, local):
    at = LANES - local
    low = first[d, rhs : rhs + rhs // 2, :].astype(F32)
    top = first[d + 1, rhs : rhs + rhs // 2, :].astype(F32)
    low = (low[0:1] * DIGIT + low[1:2])[:, at:]
    top = (top[0:1] * DIGIT + top[1:2])[:, at:]
    return jnp.concatenate([low, top], axis=1)


def columns_kernel(first, cinv, out):
    devices, piece, _ = out.shape
    total = cinv.shape[1]
    local = LANES // 2
    rhs = first.shape[1] * 2 // 3
    start = pl.multiple_of(lax.axis_index("sub") * piece, piece)
    high, low = split(cinv[pl.ds(start, piece), :])
    both = jnp.concatenate([high, low], axis=0)
    place = lax.broadcasted_iota(jnp.int32, (total, LANES), 0).astype(F32)

    def step(p, carry):
        row = pair_maps(first, 2 * p, rhs, local)
        one = jnp.where(place == row, 1.0, 0.0).astype(BF16)
        got = dot(both, one)
        out[2 * p] = jnp.concatenate([got[:piece, :local], got[piece:, :local]], axis=1).astype(BF16)
        out[2 * p + 1] = jnp.concatenate([got[:piece, local:], got[piece:, local:]], axis=1).astype(BF16)
        return carry

    lax.fori_loop(0, devices // 2, step, 0)


def restrict_kernel(sharers, got, basis, cols, out, restricted, total):
    slots, rhs, width = restricted.shape
    tail = width - LANES
    total[...] = jnp.zeros_like(total)

    def body(g, carry):
        part = None
        for u in range(GROUP):
            l = g * GROUP + u
            value = (omega(sharers, l) * unpack(got, l, rhs, tail)).astype(BF16)
            restricted[l] = value
            term = dot(value, basis[l], NT)
            part = term if part is None else part + term
        total[...] += part
        return carry

    lax.fori_loop(0, slots // GROUP, body, 0)
    high, low = split(total[...])
    block = jnp.concatenate([high, low], axis=1)

    def give(d):
        out[d, 0:rhs, :] = block
        out[d, rhs:, :] = cols[d]

    loop(slots, give)


def local_kernel(restricted, inv, out):
    def step(l):
        out[l] = dot(restricted[l], inv[l], NT)

    loop(out.shape[0], step)


def correct_kernel(groups, rows, sharers, got, first, near, basis, out, sums):
    slots, rhs, width = near.shape
    local = basis.shape[1]
    total = sums.shape[1]
    piece = got.shape[1] - rhs
    sums[...] = jnp.zeros_like(sums)
    q = lax.broadcasted_iota(jnp.int32, (total, LANES), 0)
    device = q // piece
    place = ((device % groups) * rows + (device // groups) * piece + q % piece).astype(F32)
    lane = lax.broadcasted_iota(jnp.int32, (rhs, LANES), 1)

    def step(p, carry):
        row = pair_maps(first, 2 * p, rhs, local)
        one = jnp.where(place == row, 1.0, 0.0).astype(BF16)
        a = got[2 * p, 0:rhs, :].astype(F32)
        b = got[2 * p + 1, 0:rhs, :].astype(F32)
        high = jnp.where(lane < local, a, pltpu.roll(b, local, 1))
        low = jnp.where(lane < local, pltpu.roll(a, local, 1), b)
        sums[...] += dot(jnp.concatenate([high, low], axis=0).astype(BF16), one, NT)
        return carry

    lax.fori_loop(0, slots // 2, step, 0)
    high, low = split(sums[0:rhs, :] + sums[rhs:, :])
    columns = got[:, rhs:, :].reshape(total, LANES)
    prod = dot(jnp.concatenate([high, low], axis=0), columns)
    picked = (prod[:rhs, :local] + prod[:rhs, local:] + prod[rhs:, :local]).astype(BF16)
    extra = jnp.zeros((rhs // 2, LANES), F32)

    def finish(l):
        value = dot(picked, basis[l]) + near[l]
        pack(out, l, omega(sharers, l) * value, extra)

    loop(slots, finish)


def inner_kernel(inner, inv, out):
    for u in range(out.shape[0]):
        out[u] = dot(inner[u], inv[u], NT)


def joint_kernel(elem, couple, inv, out):
    def step(l):
        out[l] = dot(couple[l], inv[elem[0, l]], NT).astype(BF16)

    loop(out.shape[0], step, 2)


def extend_kernel(elem, got, joint, base, inner_out, face_out, sums):
    slots, rhs, width = face_out.shape
    tail = width - LANES
    sums[...] = base[...]

    def step(l):
        value = unpack(got, l, rhs, tail).astype(BF16)
        face_out[l] = value
        sums[elem[0, l]] -= dot(value, joint[l])

    loop(slots, step)
    inner_out[...] = sums[...].astype(BF16)


def call(kernel, out_shape, in_specs, scratch=(), flops=0, limit=None, name=None):
    many = isinstance(out_shape, (tuple, list))
    return pl.pallas_call(
        kernel,
        out_shape=out_shape,
        in_specs=in_specs,
        out_specs=tuple(VMEM for _ in out_shape) if many else VMEM,
        scratch_shapes=list(scratch),
        cost_estimate=pl.CostEstimate(flops=flops, bytes_accessed=flops // 16, transcendentals=0),
        compiler_params=pltpu.CompilerParams(vmem_limit_bytes=limit) if limit else None,
        name=name,
    )


def body(
    res_inner,
    res_face,
    inner_inv,
    face_coupling,
    face_elem,
    face_inv,
    coarse_basis,
    coarse_map,
    coarse_inv,
    recv_index,
    sharers,
):
    slots, rhs, width = res_face.shape
    owned = slots // 4
    elements = res_inner.shape[0]
    rows, total = coarse_inv.shape
    groups = total // rows
    piece = rows * groups // slots
    shape = jax.ShapeDtypeStruct
    block_rows = rhs + rhs // 2
    wire = shape((slots, block_rows, LANES), BF16)
    unit = 2 * rhs * width * width

    sent = call(
        condense_kernel,
        wire,
        [SMEM, SMEM, VMEM, ANY, ANY, ANY, ANY],
        [
            pltpu.VMEM((slots, rhs, width), BF16),
            pltpu.VMEM((slots, width, width), BF16),
            pltpu.VMEM((slots, width, width), BF16),
            pltpu.VMEM((slots, rhs, width), BF16),
            pltpu.SemaphoreType.DMA((4, slots)),
        ],
        flops=2 * slots * unit,
        name="condense",
    )(face_elem, sharers, coarse_map, res_inner, inner_inv, face_coupling, res_face)
    first = exchange(sent)

    owner = call(
        owner_kernel,
        wire,
        [SMEM, VMEM],
        [pltpu.VMEM((owned + 1, block_rows, LANES), F32), pltpu.VMEM((owned + 1, block_rows, LANES), BF16)],
        flops=slots * block_rows * LANES,
        name="owner",
    )
    inner_w = pl.pallas_call(
        inner_kernel,
        out_shape=shape((elements, rhs, width), F32),
        grid=(elements // GROUP,),
        in_specs=[
            pl.BlockSpec((GROUP, rhs, width), lambda i: (i, 0, 0)),
            pl.BlockSpec((GROUP, width, width), lambda i: (i, 0, 0)),
        ],
        out_specs=pl.BlockSpec((GROUP, rhs, width), lambda i: (i, 0, 0)),
        cost_estimate=pl.CostEstimate(flops=elements * unit, bytes_accessed=6 << 20, transcendentals=0),
        name="inner",
    )(res_inner, inner_inv)
    joint = call(
        joint_kernel, shape((slots, width, width), BF16), [SMEM, VMEM, VMEM], flops=9 * slots * unit, name="joint"
    )(face_elem, face_coupling, inner_inv)

    gathered = exchange(owner(recv_index, first))
    columns = call(
        columns_kernel,
        shape((slots, piece, LANES), BF16),
        [VMEM, VMEM],
        flops=4 * piece * total * slots * LANES // 2,
        name="columns",
    )(first, coarse_inv)
    coarse, restricted = call(
        restrict_kernel,
        (shape((slots, rhs + piece, LANES), BF16), shape((slots, rhs, width), BF16)),
        [SMEM, VMEM, VMEM, VMEM],
        [pltpu.VMEM((rhs, coarse_map.shape[1]), F32)],
        flops=slots * unit // 2,
        name="restrict",
    )(sharers, gathered, coarse_basis, columns)
    every = exchange(coarse)
    near = call(
        local_kernel, shape((slots, rhs, width), F32), [VMEM, VMEM], flops=slots * unit, name="local"
    )(restricted, face_inv)
    weighted = call(
        functools.partial(correct_kernel, groups, rows),
        wire,
        [SMEM, VMEM, VMEM, VMEM, VMEM],
        [pltpu.VMEM((2 * rhs, total), F32)],
        flops=slots * unit // 2,
        name="correct",
    )(sharers, every, first, near, coarse_basis)
    assembled = exchange(owner(recv_index, exchange(weighted)))
    return call(
        extend_kernel,
        (shape((elements, rhs, width), BF16), shape((slots, rhs, width), BF16)),
        [SMEM, VMEM, VMEM, VMEM],
        [pltpu.VMEM((elements, rhs, width), F32)],
        flops=slots * unit,
        name="extend",
    )(face_elem, assembled, joint, inner_w)


def solution(mesh):
    block = P(AXES, None, None)
    row = P(AXES, None)
    return jax.shard_map(
        body,
        mesh=mesh,
        in_specs=(block, block, block, block, row, block, block, row, P("grp", None), row, row),
        out_specs=(block, block),
        check_vma=False,
    )
```

```python
import functools

import jax
import jax.numpy as jnp
from jax import lax
from jax.experimental import pallas as pl
from jax.experimental.pallas import tpu as pltpu
from jax.sharding import PartitionSpec as P

AXES = ("sub", "grp")
DIGIT = 128
LANES = 128
NT = (((1,), (1,)), ((), ()))
NN = (((1,), (0,)), ((), ()))
F32 = jnp.float32
BF16 = jnp.bfloat16
VMEM = pl.BlockSpec(memory_space=pltpu.VMEM)
SMEM = pl.BlockSpec(memory_space=pltpu.SMEM)
HBM = pl.BlockSpec(memory_space=pltpu.HBM)
CHUNK = 16


def exchange(blocks):
    return lax.all_to_all(blocks, AXES, split_axis=0, concat_axis=0, tiled=True)


def dot(a, b, dims=NN):
    return lax.dot_general(a, b, dims, preferred_element_type=F32)


def omega(sharers, slot):
    count = sharers[0, slot]
    return jnp.where(count > 0, 1.0 / jnp.maximum(count, 1).astype(F32), 0.0)


def split(value):
    high = value.astype(BF16)
    return high, (value - high.astype(F32)).astype(BF16)


def pack(out, slot, value, extra):
    rhs, width = value.shape
    tail = width - LANES
    half = rhs // 2
    out[slot, 0:rhs, :] = value[:, :LANES].astype(BF16)
    end = value[:, LANES:]
    out[slot, rhs : rhs + half, :] = jnp.concatenate(
        [end[:half], end[half:], extra[:, 2 * tail :]], axis=1
    ).astype(BF16)


def unpack(ref, slot, rhs, tail):
    half = rhs // 2
    main = ref[slot, 0:rhs, :].astype(F32)
    last = ref[slot, rhs : rhs + half, :].astype(F32)
    end = jnp.concatenate([last[:, :tail], last[:, tail : 2 * tail]], axis=0)
    return jnp.concatenate([main, end], axis=1)


def loop(count, step, group=16):
    group = min(group, count)

    def body(g, carry):
        for u in range(group):
            step(g * group + u)
        return carry

    lax.fori_loop(0, count // group, body, 0)


def condense_kernel(
    elem_in, sharers_in, cmap, inner, inv, couple, face, out, elem, sharers, rin, invs, cps, fac, sems, small
):
    slots, rhs, width = fac.shape
    tail = width - LANES
    chunks = slots // CHUNK

    def inner_copy(l):
        return pltpu.make_async_copy(inner.at[elem[0, l]], rin.at[l], sems.at[0, l])

    def inv_copy(l):
        return pltpu.make_async_copy(inv.at[elem[0, l]], invs.at[l], sems.at[1, l])

    def couple_copy(c):
        part = pl.ds(c * CHUNK, CHUNK)
        return pltpu.make_async_copy(couple.at[part], cps.at[part], sems.at[2, c])

    def face_copy(c):
        part = pl.ds(c * CHUNK, CHUNK)
        return pltpu.make_async_copy(face.at[part], fac.at[part], sems.at[3, c])

    elem_copy = pltpu.make_async_copy(elem_in, elem, small.at[0])
    sharers_copy = pltpu.make_async_copy(sharers_in, sharers, small.at[1])
    elem_copy.start()
    sharers_copy.start()
    elem_copy.wait()

    def start(c, carry):
        for u in range(CHUNK):
            inner_copy(c * CHUNK + u).start()
            inv_copy(c * CHUNK + u).start()
        couple_copy(c).start()
        face_copy(c).start()
        return carry

    lax.fori_loop(0, chunks, start, 0)
    maps = cmap[...]
    digits = jnp.concatenate([maps // DIGIT, maps % DIGIT], axis=0).astype(F32)
    local = digits.shape[1]
    digits = jnp.concatenate([digits, jnp.zeros((rhs // 2 - 2, local), F32)], axis=0)
    extra = jnp.concatenate([jnp.zeros((rhs // 2, LANES - local), F32), digits], axis=1)
    sharers_copy.wait()

    def chunk(c, carry):
        for u in range(CHUNK):
            inner_copy(c * CHUNK + u).wait()
            inv_copy(c * CHUNK + u).wait()
        couple_copy(c).wait()
        face_copy(c).wait()
        for u in range(CHUNK):
            l = c * CHUNK + u
            near = dot(rin[l], invs[l], NT).astype(BF16)
            value = fac[l].astype(F32) - dot(near, cps[l], NT)
            pack(out, l, omega(sharers, l) * value, extra)
        return carry

    lax.fori_loop(0, chunks, chunk, 0)


def assemble(recv, got, out, sums, rounded):
    slots = got.shape[0]
    rows = sums.shape[1]
    owned = sums.shape[0] - 1
    sums[...] = jnp.zeros_like(sums)

    def add(s):
        j = recv[0, s]
        sums[j] += got[s, :rows, :].astype(F32)

    loop(slots, add)
    rounded[...] = sums[...].astype(BF16)
    rounded[owned] = jnp.zeros(rounded.shape[1:], BF16)

    def give(s):
        out[s, :rows, :] = rounded[recv[0, s]]

    loop(slots, give)


def pair_digits(first, d, rhs, local):
    at = LANES - local
    low = first[d, rhs : rhs + rhs // 2, :].astype(F32)
    top = first[d + 1, rhs : rhs + rhs // 2, :].astype(F32)
    both = jnp.concatenate([low[:, at:], top[:, at:]], axis=1).astype(jnp.int32)
    return both[0:1], both[1:2]


def take_lanes(ref, tile, lane):
    rows, total = ref.shape
    lane = jnp.broadcast_to(lane, (rows, LANES))
    tile = jnp.broadcast_to(tile, (rows, LANES))
    taken = None
    for t in range(total // LANES):
        part = jnp.take_along_axis(ref[:, t * LANES : (t + 1) * LANES], lane, axis=1)
        taken = part if taken is None else jnp.where(tile == t, part, taken)
    return taken


def owner_kernel(recv, got, out, sums, rounded):
    assemble(recv, got, out, sums, rounded)


def first_owner_kernel(recv, got, cinv, out, sums, rounded, strip):
    slots, height, _ = out.shape
    head = got.shape[1]
    piece = height - head
    rhs = head * 2 // 3
    local = LANES // 2
    assemble(recv, got, out, sums, rounded)
    start = pl.multiple_of(lax.axis_index("sub") * piece, piece)
    strip[...] = cinv[pl.ds(start, piece), :]
    left = lax.broadcasted_iota(jnp.int32, (piece, LANES), 1) < local

    def step(p):
        taken = take_lanes(strip, *pair_digits(got, 2 * p, rhs, local))
        high = taken.astype(BF16).astype(F32)
        low = taken - high
        out[2 * p, head:, :] = jnp.where(left, high, pltpu.roll(low, local, 1)).astype(BF16)
        out[2 * p + 1, head:, :] = jnp.where(left, pltpu.roll(high, local, 1), low).astype(BF16)

    loop(slots // 2, step, 8)


def restrict_kernel(sharers, got, basis, out, restricted, total):
    slots, rhs, width = restricted.shape
    tail = width - LANES
    group = min(slots, 16)
    total[...] = jnp.zeros_like(total)

    def body(g, carry):
        part = None
        for u in range(group):
            l = g * group + u
            value = (omega(sharers, l) * unpack(got, l, rhs, tail)).astype(BF16)
            restricted[l] = value
            term = dot(value, basis[l], NT)
            part = term if part is None else part + term
        total[...] += part
        return carry

    lax.fori_loop(0, slots // group, body, 0)
    high, low = split(total[...])
    block = jnp.concatenate([high, low], axis=1)

    def give(d):
        out[d] = block

    loop(slots, give)


def turn_columns(groups, rows, got, head, piece, turned):
    local, total = turned.shape
    for t in range(total // LANES):
        parts = []
        for k in range(t * LANES, (t + 1) * LANES, piece):
            device = (k % rows) // piece * groups + k // rows
            parts.append(got[device, head:, :].astype(F32))
        part = jnp.concatenate(parts, axis=0)
        part = part + pltpu.roll(part, local, 1)
        turned[:, t * LANES : (t + 1) * LANES] = part.T[:local]


def correct_kernel(groups, rows, sharers, got, first, second, restricted, inv, basis, out, turned, sums):
    slots, rhs, width = restricted.shape
    head = first.shape[1]
    local = basis.shape[1]
    turn_columns(groups, rows, second, head, second.shape[1] - head, turned)
    sums[...] = jnp.zeros_like(sums)
    left = lax.broadcasted_iota(jnp.int32, (rhs, LANES), 1) < local
    group = min(slots // 2, 4)

    def body(g, carry):
        part = None
        for u in range(group):
            p = g * group + u
            columns = jnp.concatenate(split(take_lanes(turned, *pair_digits(first, 2 * p, rhs, local))), axis=0)
            a = got[2 * p].astype(F32)
            b = got[2 * p + 1].astype(F32)
            high = jnp.where(left, a, pltpu.roll(b, local, 1))
            low = jnp.where(left, pltpu.roll(a, local, 1), b)
            term = dot(jnp.concatenate([high, low], axis=0).astype(BF16), columns, NT)
            part = term if part is None else part + term
        sums[...] += part
        return carry

    lax.fori_loop(0, slots // 2 // group, body, 0)
    prod = sums[...]
    picked = (prod[:rhs, :local] + (prod[:rhs, local:] + prod[rhs:, :local])).astype(BF16)
    extra = jnp.zeros((rhs // 2, LANES), F32)

    def finish(l):
        value = dot(picked, basis[l]) + dot(restricted[l], inv[l], NT)
        pack(out, l, omega(sharers, l) * value, extra)

    loop(slots, finish)


def extend_kernel(elem, got, inner, couple, inv, inner_out, face_out, sums):
    slots, rhs, width = face_out.shape
    tail = width - LANES
    sums[...] = inner[...].astype(F32)

    def step(l):
        value = unpack(got, l, rhs, tail).astype(BF16)
        face_out[l] = value
        sums[elem[0, l]] -= dot(value, couple[l])

    loop(slots, step)

    def finish(e):
        inner_out[e] = dot(sums[e].astype(BF16), inv[e], NT).astype(BF16)

    loop(inner_out.shape[0], finish)


def padded(shape, dtype):
    size = jnp.dtype(dtype).itemsize
    for n in shape[:-2]:
        size *= n
    return size * (-(-shape[-2] // 16) * 16) * (-(-shape[-1] // LANES) * LANES)


def call(kernel, out_shape, specs, args, scratch=(), flops=0, name=None, limit=None):
    many = isinstance(out_shape, (tuple, list))
    outs = tuple(out_shape) if many else (out_shape,)
    held = [a for a, s in zip(args, specs) if s is VMEM] + list(outs)
    need = sum(padded(a.shape, a.dtype) for a in held)
    room = sum(padded(shape, dtype) for shape, dtype in scratch if dtype is not None)
    made = [pltpu.VMEM(shape, dtype) if dtype is not None else shape for shape, dtype in scratch]
    return pl.pallas_call(
        kernel,
        out_shape=out_shape,
        in_specs=specs,
        out_specs=tuple(VMEM for _ in outs) if many else VMEM,
        scratch_shapes=made,
        cost_estimate=pl.CostEstimate(flops=flops, bytes_accessed=need, transcendentals=0),
        compiler_params=pltpu.CompilerParams(vmem_limit_bytes=limit or need + room + (2 << 20)),
        name=name,
    )(*args)


def body(
    res_inner,
    res_face,
    inner_inv,
    face_coupling,
    face_elem,
    face_inv,
    coarse_basis,
    coarse_map,
    coarse_inv,
    recv_index,
    sharers,
):
    slots, rhs, width = res_face.shape
    owned = slots // 4
    elements = res_inner.shape[0]
    rows, total = coarse_inv.shape
    local = coarse_map.shape[1]
    groups = total // rows
    piece = rows * groups // slots
    shape = jax.ShapeDtypeStruct
    head = rhs + rhs // 2
    wire = shape((slots, head, LANES), BF16)
    unit = 2 * rhs * width * width
    tables = [((owned + 1, head, LANES), F32), ((owned + 1, head, LANES), BF16)]

    sent = call(
        condense_kernel,
        wire,
        [HBM, HBM, VMEM, HBM, HBM, HBM, HBM],
        (face_elem, sharers, coarse_map, res_inner, inner_inv, face_coupling, res_face),
        [
            (pltpu.SMEM(face_elem.shape, jnp.int32), None),
            (pltpu.SMEM(sharers.shape, jnp.int32), None),
            ((slots, rhs, width), BF16),
            ((slots, width, width), BF16),
            ((slots, width, width), BF16),
            ((slots, rhs, width), BF16),
            (pltpu.SemaphoreType.DMA((4, slots)), None),
            (pltpu.SemaphoreType.DMA((2,)), None),
        ],
        flops=2 * slots * unit,
        name="condense",
        limit=60 * 1024 * 1024,
    )
    first = exchange(sent)
    held = call(
        first_owner_kernel,
        shape((slots, head + piece, LANES), BF16),
        [SMEM, VMEM, VMEM],
        (recv_index, first, coarse_inv),
        tables + [((piece, total), F32)],
        flops=slots * head * LANES,
        name="first_owner",
    )
    gathered = exchange(held)
    coarse, restricted = call(
        restrict_kernel,
        (shape((slots, rhs, LANES), BF16), shape((slots, rhs, width), BF16)),
        [SMEM, VMEM, VMEM],
        (sharers, gathered, coarse_basis),
        [((rhs, local), F32)],
        flops=slots * unit // 2,
        name="restrict",
    )
    every = exchange(coarse)
    weighted = call(
        functools.partial(correct_kernel, groups, rows),
        wire,
        [SMEM, VMEM, VMEM, VMEM, VMEM, VMEM, VMEM],
        (sharers, every, first, gathered, restricted, face_inv, coarse_basis),
        [((local, total), F32), ((2 * rhs, LANES), F32)],
        flops=2 * slots * unit,
        name="correct",
    )
    third = exchange(weighted)
    spread = call(
        owner_kernel, wire, [SMEM, VMEM], (recv_index, third), tables, flops=slots * head * LANES, name="owner"
    )
    assembled = exchange(spread)
    return call(
        extend_kernel,
        (shape((elements, rhs, width), BF16), shape((slots, rhs, width), BF16)),
        [SMEM, VMEM, VMEM, VMEM, VMEM],
        (face_elem, assembled, res_inner, face_coupling, inner_inv),
        [((elements, rhs, width), F32)],
        flops=2 * slots * unit,
        name="extend",
    )


def solution(mesh):
    block = P(AXES, None, None)
    row = P(AXES, None)
    return jax.shard_map(
        body,
        mesh=mesh,
        in_specs=(block, block, block, block, row, block, block, row, P("grp", None), row, row),
        out_specs=(block, block),
        check_vma=False,
    )
```

```python
import functools

import jax
import jax.numpy as jnp
from jax import lax
from jax.experimental import pallas as pl
from jax.experimental.pallas import tpu as pltpu
from jax.sharding import PartitionSpec as P

AXES = ("sub", "grp")
DIGIT = 128
LANES = 128
NT = (((1,), (1,)), ((), ()))
NN = (((1,), (0,)), ((), ()))
F32 = jnp.float32
BF16 = jnp.bfloat16
VMEM = pl.BlockSpec(memory_space=pltpu.VMEM)
SMEM = pl.BlockSpec(memory_space=pltpu.SMEM)
HBM = pl.BlockSpec(memory_space=pltpu.HBM)
CHUNK = 16


def exchange(blocks):
    return lax.all_to_all(blocks, AXES, split_axis=0, concat_axis=0, tiled=True)


def dot(a, b, dims=NN):
    return lax.dot_general(a, b, dims, preferred_element_type=F32)


def omega(sharers, slot):
    count = sharers[0, slot]
    return jnp.where(count > 0, 1.0 / jnp.maximum(count, 1).astype(F32), 0.0)


def pack(out, slot, value, extra):
    rhs, width = value.shape
    tail = width - LANES
    half = rhs // 2
    out[slot, 0:rhs, :] = value[:, :LANES].astype(BF16)
    end = value[:, LANES:]
    out[slot, rhs : rhs + half, :] = jnp.concatenate(
        [end[:half], end[half:], extra[:, 2 * tail :]], axis=1
    ).astype(BF16)


def unpack(ref, slot, rhs, tail):
    half = rhs // 2
    main = ref[slot, 0:rhs, :].astype(F32)
    last = ref[slot, rhs : rhs + half, :].astype(F32)
    end = jnp.concatenate([last[:, :tail], last[:, tail : 2 * tail]], axis=0)
    return jnp.concatenate([main, end], axis=1)


def loop(count, step, group=16):
    group = min(group, count)

    def body(g, carry):
        for u in range(group):
            step(g * group + u)
        return carry

    lax.fori_loop(0, count // group, body, 0)


def condense_kernel(
    elem_in, sharers_in, map_in, inner, inv, couple, face, out, elem, sharers, cmap, rin, invs, cps, fac, stage, sems, small
):
    slots, rhs, width = fac.shape
    step = min(slots, CHUNK)
    chunks = slots // step
    copy = pltpu.make_async_copy

    def part(c):
        return pl.ds(c * step, step)

    def couple_copy(c):
        return copy(couple.at[part(c)], cps.at[part(c)], sems.at[2, c])

    def face_copy(c):
        return copy(face.at[part(c)], fac.at[part(c)], sems.at[3, c])

    def out_copy(c):
        return copy(stage.at[part(c)], out.at[part(c)], sems.at[4, c])

    first = copy(elem_in, elem, small.at[0])
    others = [copy(sharers_in, sharers, small.at[1]), copy(map_in, cmap, small.at[2])]
    first.start()
    for other in others:
        other.start()
    couple_copy(0).start()
    face_copy(0).start()
    first.wait()
    for c in range(chunks):
        for u in range(step):
            l = c * step + u
            copy(inner.at[elem[0, l]], rin.at[l], sems.at[0, c]).start()
            copy(inv.at[elem[0, l]], invs.at[l], sems.at[1, c]).start()
        if c > 0:
            couple_copy(c).start()
            face_copy(c).start()
    for other in others:
        other.wait()
    maps = cmap[...]
    digits = jnp.concatenate([maps // DIGIT, maps % DIGIT], axis=0).astype(F32)
    local = digits.shape[1]
    digits = jnp.concatenate([digits, jnp.zeros((rhs // 2 - 2, local), F32)], axis=0)
    extra = jnp.concatenate([jnp.zeros((rhs // 2, LANES - local), F32), digits], axis=1)
    for c in range(chunks):
        copy(inner.at[pl.ds(0, step)], rin.at[part(c)], sems.at[0, c]).wait()
        copy(inv.at[pl.ds(0, step)], invs.at[part(c)], sems.at[1, c]).wait()
        near = [dot(rin[c * step + u], invs[c * step + u], NT).astype(BF16) for u in range(step)]
        couple_copy(c).wait()
        face_copy(c).wait()
        for u in range(step):
            l = c * step + u
            value = fac[l].astype(F32) - dot(near[u], cps[l], NT)
            pack(stage, l, omega(sharers, l) * value, extra)
        out_copy(c).start()
    for c in range(chunks):
        out_copy(c).wait()


def assemble(recv, got, out, sums, rounded):
    slots = got.shape[0]
    rows = sums.shape[1]
    owned = sums.shape[0] - 1
    sums[...] = jnp.zeros_like(sums)

    def add(s):
        j = recv[0, s]
        sums[j] += got[s, :rows, :].astype(F32)

    loop(slots, add)
    rounded[...] = sums[...].astype(BF16)
    rounded[owned] = jnp.zeros(rounded.shape[1:], BF16)

    def give(s):
        out[s, :rows, :] = rounded[recv[0, s]]

    loop(slots, give)


def pair_digits(first, d, rhs, local):
    at = LANES - local
    low = first[d, rhs : rhs + rhs // 2, :].astype(F32)
    top = first[d + 1, rhs : rhs + rhs // 2, :].astype(F32)
    both = jnp.concatenate([low[:, at:], top[:, at:]], axis=1).astype(jnp.int32)
    return both[0:1], both[1:2]


def take_lanes(ref, tile, lane):
    rows, total = ref.shape
    lane = jnp.broadcast_to(lane, (rows, LANES))
    tile = jnp.broadcast_to(tile, (rows, LANES))
    taken = None
    for t in range(total // LANES):
        part = jnp.take_along_axis(ref[:, t * LANES : (t + 1) * LANES], lane, axis=1)
        taken = part if taken is None else jnp.where(tile == t, part, taken)
    return taken


def owner_kernel(recv, got, out, sums, rounded):
    assemble(recv, got, out, sums, rounded)


def halves(value, local, left):
    half = value.shape[0] // 2
    top, low = value[:half], value[half:]
    return jnp.where(left, top, pltpu.roll(low, local, 1)), jnp.where(left, pltpu.roll(top, local, 1), low)


def first_owner_kernel(recv, got, cinv, out, sums, rounded, strip):
    slots, height, _ = out.shape
    head = got.shape[1]
    piece = strip.shape[0]
    rhs = head * 2 // 3
    local = LANES // 2
    assemble(recv, got, out, sums, rounded)
    start = pl.multiple_of(lax.axis_index("sub") * piece, piece)
    strip[...] = cinv[pl.ds(start, piece), :]
    left = lax.broadcasted_iota(jnp.int32, (piece // 2, LANES), 1) < local

    def step(p):
        taken = take_lanes(strip, *pair_digits(got, 2 * p, rhs, local))
        low, top = halves(taken, local, left)
        out[2 * p, head:, :] = low.astype(BF16)
        out[2 * p + 1, head:, :] = top.astype(BF16)

    loop(slots // 2, step)


def restrict_kernel(sharers, got, basis, out, restricted, total):
    slots, rhs, width = restricted.shape
    tail = width - LANES
    group = min(slots, 16)
    total[...] = jnp.zeros_like(total)

    def body(g, carry):
        part = None
        for u in range(group):
            l = g * group + u
            value = (omega(sharers, l) * unpack(got, l, rhs, tail)).astype(BF16)
            restricted[l] = value
            term = dot(value, basis[l], NT)
            part = term if part is None else part + term
        total[...] += part
        return carry

    lax.fori_loop(0, slots // group, body, 0)
    both = total[...]
    block = jnp.concatenate([both[: rhs // 2], both[rhs // 2 :]], axis=1).astype(BF16)

    def give(d):
        out[d] = block

    loop(slots, give)


def turn_columns(groups, rows, got, head, piece, turned):
    local, total = turned.shape
    for t in range(total // LANES):
        parts = []
        for k in range(t * LANES, (t + 1) * LANES, piece):
            block = got[(k % rows) // piece * groups + k // rows, head:, :].astype(F32)
            parts += [block, pltpu.roll(block, local, 1)]
        turned[:, t * LANES : (t + 1) * LANES] = jnp.concatenate(parts, axis=0).T[:local]


def correct_kernel(groups, rows, sharers, got, first, second, restricted, inv, basis, out, turned, sums):
    slots, rhs, width = restricted.shape
    head = first.shape[1]
    local = basis.shape[1]
    turn_columns(groups, rows, second, head, (second.shape[1] - head) * 2, turned)
    sums[...] = jnp.zeros_like(sums)
    left = lax.broadcasted_iota(jnp.int32, (rhs // 2, LANES), 1) < local
    group = min(slots // 2, 8)

    def body(g, carry):
        part = None
        for u in range(group):
            p = g * group + u
            columns = take_lanes(turned, *pair_digits(first, 2 * p, rhs, local)).astype(BF16)
            low = got[2 * p].astype(F32)
            top = got[2 * p + 1].astype(F32)
            value = jnp.concatenate(halves(jnp.concatenate([low, top], axis=0), local, left), axis=0)
            term = dot(value.astype(BF16), columns, NT)
            part = term if part is None else part + term
        sums[...] += part
        return carry

    lax.fori_loop(0, slots // 2 // group, body, 0)
    picked = sums[...].astype(BF16)
    extra = jnp.zeros((rhs // 2, LANES), F32)

    def finish(l):
        value = dot(picked, basis[l]) + dot(restricted[l], inv[l], NT)
        pack(out, l, omega(sharers, l) * value, extra)

    loop(slots, finish)


def extend_kernel(elem, got, inner, couple, inv, inner_out, face_out, sums):
    slots, rhs, width = face_out.shape
    tail = width - LANES
    sums[...] = inner[...].astype(F32)

    def step(l):
        value = unpack(got, l, rhs, tail).astype(BF16)
        face_out[l] = value
        sums[elem[0, l]] -= dot(value, couple[l])

    loop(slots, step, 32)

    def finish(e):
        inner_out[e] = dot(sums[e].astype(BF16), inv[e], NT).astype(BF16)

    loop(inner_out.shape[0], finish, 32)


def padded(shape, dtype):
    size = jnp.dtype(dtype).itemsize
    for n in shape[:-2]:
        size *= n
    return size * (-(-shape[-2] // 16) * 16) * (-(-shape[-1] // LANES) * LANES)


def call(kernel, out_shape, specs, args, scratch=(), flops=0, name=None, limit=None, out_spec=VMEM):
    many = isinstance(out_shape, (tuple, list))
    outs = tuple(out_shape) if many else (out_shape,)
    held = [a for a, s in zip(args, specs) if s is VMEM] + list(outs)
    need = sum(padded(a.shape, a.dtype) for a in held)
    room = sum(padded(shape, dtype) for shape, dtype in scratch if dtype is not None)
    made = [pltpu.VMEM(shape, dtype) if dtype is not None else shape for shape, dtype in scratch]
    return pl.pallas_call(
        kernel,
        out_shape=out_shape,
        in_specs=specs,
        out_specs=tuple(VMEM for _ in outs) if many else out_spec,
        scratch_shapes=made,
        cost_estimate=pl.CostEstimate(flops=flops, bytes_accessed=need, transcendentals=0),
        compiler_params=pltpu.CompilerParams(vmem_limit_bytes=limit or need + room + (2 << 20)),
        name=name,
    )(*args)


def body(
    res_inner,
    res_face,
    inner_inv,
    face_coupling,
    face_elem,
    face_inv,
    coarse_basis,
    coarse_map,
    coarse_inv,
    recv_index,
    sharers,
):
    slots, rhs, width = res_face.shape
    owned = slots // 4
    elements = res_inner.shape[0]
    rows, total = coarse_inv.shape
    local = coarse_map.shape[1]
    groups = total // rows
    piece = rows * groups // slots
    shape = jax.ShapeDtypeStruct
    head = rhs + rhs // 2
    wire = shape((slots, head, LANES), BF16)
    unit = 2 * rhs * width * width
    tables = [((owned + 1, head, LANES), F32), ((owned + 1, head, LANES), BF16)]

    sent = call(
        condense_kernel,
        wire,
        [HBM] * 7,
        (face_elem, sharers, coarse_map, res_inner, inner_inv, face_coupling, res_face),
        [
            (pltpu.SMEM(face_elem.shape, jnp.int32), None),
            (pltpu.SMEM(sharers.shape, jnp.int32), None),
            (pltpu.VMEM(coarse_map.shape, jnp.int32), None),
            ((slots, rhs, width), BF16),
            ((slots, width, width), BF16),
            ((slots, width, width), BF16),
            ((slots, rhs, width), BF16),
            ((slots, head, LANES), BF16),
            (pltpu.SemaphoreType.DMA((5, -(-slots // CHUNK))), None),
            (pltpu.SemaphoreType.DMA((3,)), None),
        ],
        flops=2 * slots * unit,
        name="condense",
        limit=60 * 1024 * 1024,
        out_spec=HBM,
    )
    first = exchange(sent)
    held = call(
        first_owner_kernel,
        shape((slots, head + piece // 2, LANES), BF16),
        [SMEM, VMEM, VMEM],
        (recv_index, first, coarse_inv),
        tables + [((piece, total), F32)],
        flops=100 * slots * unit,
        name="first_owner",
    )
    gathered = exchange(held)
    coarse, restricted = call(
        restrict_kernel,
        (shape((slots, rhs // 2, LANES), BF16), shape((slots, rhs, width), BF16)),
        [SMEM, VMEM, VMEM],
        (sharers, gathered, coarse_basis),
        [((rhs, local), F32)],
        flops=100 * slots * unit,
        name="restrict",
    )
    every = exchange(coarse)
    weighted = call(
        functools.partial(correct_kernel, groups, rows),
        wire,
        [SMEM, VMEM, VMEM, VMEM, VMEM, VMEM, VMEM],
        (sharers, every, first, gathered, restricted, face_inv, coarse_basis),
        [((local, total), F32), ((rhs, local), F32)],
        flops=2 * slots * unit,
        name="correct",
    )
    third = exchange(weighted)
    spread = call(
        owner_kernel, wire, [SMEM, VMEM], (recv_index, third), tables, flops=slots * head * LANES, name="owner"
    )
    assembled = exchange(spread)
    return call(
        extend_kernel,
        (shape((elements, rhs, width), BF16), shape((slots, rhs, width), BF16)),
        [SMEM, VMEM, VMEM, VMEM, VMEM],
        (face_elem, assembled, res_inner, face_coupling, inner_inv),
        [((elements, rhs, width), F32)],
        flops=2 * slots * unit,
        name="extend",
    )


def solution(mesh):
    block = P(AXES, None, None)
    row = P(AXES, None)
    return jax.shard_map(
        body,
        mesh=mesh,
        in_specs=(block, block, block, block, row, block, block, row, P("grp", None), row, row),
        out_specs=(block, block),
        check_vma=False,
    )
```

```python
import functools

import jax
import jax.numpy as jnp
from jax import lax
from jax.experimental import pallas as pl
from jax.experimental.pallas import tpu as pltpu
from jax.sharding import PartitionSpec as P

AXES = ("sub", "grp")
DIGIT = 128
LANES = 128
NT = (((1,), (1,)), ((), ()))
NN = (((1,), (0,)), ((), ()))
F32 = jnp.float32
BF16 = jnp.bfloat16
VMEM = pl.BlockSpec(memory_space=pltpu.VMEM)
SMEM = pl.BlockSpec(memory_space=pltpu.SMEM)
HBM = pl.BlockSpec(memory_space=pltpu.HBM)
CHUNK = 16
ROWS = 4


def exchange(blocks):
    return lax.all_to_all(blocks, AXES, split_axis=0, concat_axis=0, tiled=True)


def dot(a, b, dims=NN):
    return lax.dot_general(a, b, dims, preferred_element_type=F32)


def omega(sharers, slot):
    count = sharers[0, slot]
    return jnp.where(count > 0, 1.0 / jnp.maximum(count, 1).astype(F32), 0.0)


def pack(out, slot, value, extra):
    count = value.shape[0] // ROWS
    value_rows = [value[ROWS * j : ROWS * (j + 1)] for j in range(count)]
    for j in range(count):
        out[slot, j] = value_rows[j][:, :LANES].astype(BF16)
    out[slot, count] = jnp.concatenate([v[:, LANES:] for v in value_rows] + [extra], axis=1).astype(BF16)


def unpack(ref, slot, rhs, tail):
    count = rhs // ROWS
    main = [ref[slot, j].astype(F32) for j in range(count)]
    last = ref[slot, count].astype(F32)
    end = [last[:, j * tail : (j + 1) * tail] for j in range(count)]
    return jnp.concatenate([jnp.concatenate(main, axis=0), jnp.concatenate(end, axis=0)], axis=1)


def loop(count, step, group=16):
    group = min(group, count)

    def body(g, carry):
        for u in range(group):
            step(g * group + u)
        return carry

    lax.fori_loop(0, count // group, body, 0)


def condense_kernel(
    elem_in, sharers_in, map_in, inner, inv, couple, face, out, elem, sharers, cmap, rin, invs, cps, fac, stage, sems, small
):
    slots, rhs, width = fac.shape
    step = min(slots, CHUNK)
    chunks = slots // step
    copy = pltpu.make_async_copy

    def part(c):
        return pl.ds(c * step, step)

    def couple_copy(c):
        return copy(couple.at[part(c)], cps.at[part(c)], sems.at[2, c])

    def face_copy(c):
        return copy(face.at[part(c)], fac.at[part(c)], sems.at[3, c])

    def out_copy(c):
        return copy(stage.at[part(c)], out.at[part(c)], sems.at[4, c])

    first = copy(elem_in, elem, small.at[0])
    others = [copy(sharers_in, sharers, small.at[1]), copy(map_in, cmap, small.at[2])]
    first.start()
    for other in others:
        other.start()
    couple_copy(0).start()
    face_copy(0).start()
    first.wait()
    for c in range(chunks):
        for u in range(step):
            l = c * step + u
            copy(inner.at[elem[0, l]], rin.at[l], sems.at[0, c]).start()
            copy(inv.at[elem[0, l]], invs.at[l], sems.at[1, c]).start()
        if c > 0:
            couple_copy(c).start()
            face_copy(c).start()
    for other in others:
        other.wait()
    maps = cmap[...]
    digits = jnp.concatenate([maps // DIGIT, maps % DIGIT], axis=0).astype(F32)
    local = digits.shape[1]
    spare = LANES - rhs // ROWS * (width - LANES)
    digits = jnp.concatenate([digits, jnp.zeros((ROWS - 2, local), F32)], axis=0)
    extra = jnp.concatenate([jnp.zeros((ROWS, spare - local), F32), digits], axis=1) if spare > local else digits
    for c in range(chunks):
        copy(inner.at[pl.ds(0, step)], rin.at[part(c)], sems.at[0, c]).wait()
        copy(inv.at[pl.ds(0, step)], invs.at[part(c)], sems.at[1, c]).wait()
        near = [dot(rin[c * step + u], invs[c * step + u], NT).astype(BF16) for u in range(step)]
        couple_copy(c).wait()
        face_copy(c).wait()
        for u in range(step):
            l = c * step + u
            value = fac[l].astype(F32) - dot(near[u], cps[l], NT)
            pack(stage, l, omega(sharers, l) * value, extra)
        out_copy(c).start()
    for c in range(chunks):
        out_copy(c).wait()


def assemble(recv, got, out, sums, rounded):
    slots = got.shape[0]
    rows = sums.shape[1]
    owned = sums.shape[0] - 1
    sums[...] = jnp.zeros_like(sums)

    def add(s):
        j = recv[0, s]
        sums[j] += got[s, :rows].astype(F32)

    loop(slots, add)
    rounded[...] = sums[...].astype(BF16)
    rounded[owned] = jnp.zeros(rounded.shape[1:], BF16)

    def give(s):
        out[s, :rows] = rounded[recv[0, s]]

    loop(slots, give)


def pair_digits(first, d, local):
    last = first.shape[1] - 1
    at = LANES - local
    low = first[d, last].astype(F32)
    top = first[d + 1, last].astype(F32)
    both = jnp.concatenate([low[:2, at:], top[:2, at:]], axis=1).astype(jnp.int32)
    return both[0:1], both[1:2]


def take_lanes(ref, tile, lane):
    rows, total = ref.shape
    lane = jnp.broadcast_to(lane, (rows, LANES))
    tile = jnp.broadcast_to(tile, (rows, LANES))
    taken = None
    for t in range(total // LANES):
        part = jnp.take_along_axis(ref[:, t * LANES : (t + 1) * LANES], lane, axis=1)
        taken = part if taken is None else jnp.where(tile == t, part, taken)
    return taken


def owner_kernel(recv, got, out, sums, rounded):
    assemble(recv, got, out, sums, rounded)


def halves(value, local, left):
    half = value.shape[0] // 2
    top, low = value[:half], value[half:]
    return jnp.where(left, top, pltpu.roll(low, local, 1)), jnp.where(left, pltpu.roll(top, local, 1), low)


def first_owner_kernel(recv, got, cinv, out, sums, rounded, strip):
    slots, height, _, _ = out.shape
    head = got.shape[1]
    piece = strip.shape[0]
    local = LANES // 2
    assemble(recv, got, out, sums, rounded)
    start = pl.multiple_of(lax.axis_index("sub") * piece, piece)
    strip[...] = cinv[pl.ds(start, piece), :]
    left = lax.broadcasted_iota(jnp.int32, (piece // 2, LANES), 1) < local

    def step(p):
        taken = take_lanes(strip, *pair_digits(got, 2 * p, local))
        low, top = halves(taken, local, left)
        for j in range(height - head):
            out[2 * p, head + j] = low[ROWS * j : ROWS * (j + 1)].astype(BF16)
            out[2 * p + 1, head + j] = top[ROWS * j : ROWS * (j + 1)].astype(BF16)

    loop(slots // 2, step)


def restrict_kernel(sharers, got, basis, out, restricted, total):
    slots, rhs, width = restricted.shape
    tail = width - LANES
    group = min(slots, 16)
    total[...] = jnp.zeros_like(total)

    def body(g, carry):
        part = None
        for u in range(group):
            l = g * group + u
            value = (omega(sharers, l) * unpack(got, l, rhs, tail)).astype(BF16)
            restricted[l] = value
            term = dot(value, basis[l], NT)
            part = term if part is None else part + term
        total[...] += part
        return carry

    lax.fori_loop(0, slots // group, body, 0)
    both = total[...]
    block = jnp.concatenate([both[: rhs // 2], both[rhs // 2 :]], axis=1).astype(BF16)

    def give(d):
        out[d] = block

    loop(slots, give)


def turn_columns(groups, rows, got, head, turned):
    local, total = turned.shape
    piece = (got.shape[1] - head) * ROWS * 2
    for t in range(total // LANES):
        parts = []
        for k in range(t * LANES, (t + 1) * LANES, piece):
            device = (k % rows) // piece * groups + k // rows
            block = [got[device, j].astype(F32) for j in range(head, got.shape[1])]
            block = jnp.concatenate(block, axis=0)
            parts += [block, pltpu.roll(block, local, 1)]
        turned[:, t * LANES : (t + 1) * LANES] = jnp.concatenate(parts, axis=0).T[:local]


def correct_kernel(groups, rows, sharers, got, first, second, restricted, inv, basis, out, turned, sums):
    slots, rhs, width = restricted.shape
    head = first.shape[1]
    local = basis.shape[1]
    turn_columns(groups, rows, second, head, turned)
    sums[...] = jnp.zeros_like(sums)
    left = lax.broadcasted_iota(jnp.int32, (rhs // 2, LANES), 1) < local
    group = min(slots // 2, 8)

    def body(g, carry):
        part = None
        for u in range(group):
            p = g * group + u
            columns = take_lanes(turned, *pair_digits(first, 2 * p, local)).astype(BF16)
            low = got[2 * p].astype(F32)
            top = got[2 * p + 1].astype(F32)
            value = jnp.concatenate(halves(jnp.concatenate([low, top], axis=0), local, left), axis=0)
            term = dot(value.astype(BF16), columns, NT)
            part = term if part is None else part + term
        sums[...] += part
        return carry

    lax.fori_loop(0, slots // 2 // group, body, 0)
    picked = sums[...].astype(BF16)
    extra = jnp.zeros((ROWS, LANES - rhs // ROWS * (width - LANES)), F32)

    def finish(l):
        value = dot(picked, basis[l]) + dot(restricted[l], inv[l], NT)
        pack(out, l, omega(sharers, l) * value, extra)

    loop(slots, finish)


def extend_kernel(elem, got, inner, couple, inv, inner_out, face_out, sums):
    slots, rhs, width = face_out.shape
    tail = width - LANES
    sums[...] = inner[...].astype(F32)

    def step(l):
        value = unpack(got, l, rhs, tail).astype(BF16)
        face_out[l] = value
        sums[elem[0, l]] -= dot(value, couple[l])

    loop(slots, step, 32)

    def finish(e):
        inner_out[e] = dot(sums[e].astype(BF16), inv[e], NT).astype(BF16)

    loop(inner_out.shape[0], finish, 32)


def padded(shape, dtype):
    size = jnp.dtype(dtype).itemsize
    for n in shape[:-2]:
        size *= n
    high = shape[-2] if shape[-2] < 8 else -(-shape[-2] // 16) * 16
    return size * high * (-(-shape[-1] // LANES) * LANES)


def call(kernel, out_shape, specs, args, scratch=(), flops=0, name=None, limit=None, out_spec=VMEM):
    many = isinstance(out_shape, (tuple, list))
    outs = tuple(out_shape) if many else (out_shape,)
    held = [a for a, s in zip(args, specs) if s is VMEM] + list(outs)
    need = sum(padded(a.shape, a.dtype) for a in held)
    room = sum(padded(shape, dtype) for shape, dtype in scratch if dtype is not None)
    made = [pltpu.VMEM(shape, dtype) if dtype is not None else shape for shape, dtype in scratch]
    return pl.pallas_call(
        kernel,
        out_shape=out_shape,
        in_specs=specs,
        out_specs=tuple(VMEM for _ in outs) if many else out_spec,
        scratch_shapes=made,
        cost_estimate=pl.CostEstimate(flops=flops, bytes_accessed=need, transcendentals=0),
        compiler_params=pltpu.CompilerParams(vmem_limit_bytes=limit or need + room + (2 << 20)),
        name=name,
    )(*args)


def body(
    res_inner,
    res_face,
    inner_inv,
    face_coupling,
    face_elem,
    face_inv,
    coarse_basis,
    coarse_map,
    coarse_inv,
    recv_index,
    sharers,
):
    slots, rhs, width = res_face.shape
    owned = slots // 4
    elements = res_inner.shape[0]
    rows, total = coarse_inv.shape
    local = coarse_map.shape[1]
    groups = total // rows
    piece = rows * groups // slots
    shape = jax.ShapeDtypeStruct
    head = rhs // ROWS + 1
    wire = shape((slots, head, ROWS, LANES), BF16)
    unit = 2 * rhs * width * width
    tables = [((owned + 1, head, ROWS, LANES), F32), ((owned + 1, head, ROWS, LANES), BF16)]

    sent = call(
        condense_kernel,
        wire,
        [HBM] * 7,
        (face_elem, sharers, coarse_map, res_inner, inner_inv, face_coupling, res_face),
        [
            (pltpu.SMEM(face_elem.shape, jnp.int32), None),
            (pltpu.SMEM(sharers.shape, jnp.int32), None),
            (pltpu.VMEM(coarse_map.shape, jnp.int32), None),
            ((slots, rhs, width), BF16),
            ((slots, width, width), BF16),
            ((slots, width, width), BF16),
            ((slots, rhs, width), BF16),
            (wire.shape, BF16),
            (pltpu.SemaphoreType.DMA((5, -(-slots // CHUNK))), None),
            (pltpu.SemaphoreType.DMA((3,)), None),
        ],
        flops=2 * slots * unit,
        name="condense",
        limit=60 * 1024 * 1024,
        out_spec=HBM,
    )
    first = exchange(sent)
    held = call(
        first_owner_kernel,
        shape((slots, head + piece // (2 * ROWS), ROWS, LANES), BF16),
        [SMEM, VMEM, VMEM],
        (recv_index, first, coarse_inv),
        tables + [((piece, total), F32)],
        flops=100 * slots * unit,
        name="first_owner",
    )
    gathered = exchange(held)
    coarse, restricted = call(
        restrict_kernel,
        (shape((slots, rhs // 2, LANES), BF16), shape((slots, rhs, width), BF16)),
        [SMEM, VMEM, VMEM],
        (sharers, gathered, coarse_basis),
        [((rhs, local), F32)],
        flops=100 * slots * unit,
        name="restrict",
    )
    every = exchange(coarse)
    weighted = call(
        functools.partial(correct_kernel, groups, rows),
        wire,
        [SMEM, VMEM, VMEM, VMEM, VMEM, VMEM, VMEM],
        (sharers, every, first, gathered, restricted, face_inv, coarse_basis),
        [((local, total), F32), ((rhs, local), F32)],
        flops=2 * slots * unit,
        name="correct",
    )
    third = exchange(weighted)
    spread = call(
        owner_kernel, wire, [SMEM, VMEM], (recv_index, third), tables, flops=slots * width * LANES, name="owner"
    )
    assembled = exchange(spread)
    return call(
        extend_kernel,
        (shape((elements, rhs, width), BF16), shape((slots, rhs, width), BF16)),
        [SMEM, VMEM, VMEM, VMEM, VMEM],
        (face_elem, assembled, res_inner, face_coupling, inner_inv),
        [((elements, rhs, width), F32)],
        flops=2 * slots * unit,
        name="extend",
    )


def solution(mesh):
    block = P(AXES, None, None)
    row = P(AXES, None)
    return jax.shard_map(
        body,
        mesh=mesh,
        in_specs=(block, block, block, block, row, block, block, row, P("grp", None), row, row),
        out_specs=(block, block),
        check_vma=False,
    )
```

```python
import functools

import jax
import jax.numpy as jnp
from jax import lax
from jax.experimental import pallas as pl
from jax.experimental.pallas import tpu as pltpu
from jax.sharding import PartitionSpec as P

AXES = ("sub", "grp")
DIGIT = 128
LANES = 128
NT = (((1,), (1,)), ((), ()))
NN = (((1,), (0,)), ((), ()))
F32 = jnp.float32
BF16 = jnp.bfloat16
VMEM = pl.BlockSpec(memory_space=pltpu.VMEM)
SMEM = pl.BlockSpec(memory_space=pltpu.SMEM)
HBM = pl.BlockSpec(memory_space=pltpu.HBM)
CHUNK = 16
ROWS = 4


def exchange(blocks):
    return lax.all_to_all(blocks, AXES, split_axis=0, concat_axis=0, tiled=True)


def dot(a, b, dims=NN):
    return lax.dot_general(a, b, dims, preferred_element_type=F32)


def omega(sharers, slot):
    count = sharers[0, slot]
    return jnp.where(count > 0, 1.0 / jnp.maximum(count, 1).astype(F32), 0.0)


def pack(out, slot, value, extra):
    count = value.shape[0] // ROWS
    value_rows = [value[ROWS * j : ROWS * (j + 1)] for j in range(count)]
    for j in range(count):
        out[slot, j] = value_rows[j][:, :LANES].astype(BF16)
    out[slot, count] = jnp.concatenate([v[:, LANES:] for v in value_rows] + [extra], axis=1).astype(BF16)


def unpack(ref, slot, rhs, tail):
    count = rhs // ROWS
    main = [ref[slot, j].astype(F32) for j in range(count)]
    last = ref[slot, count].astype(F32)
    end = [last[:, j * tail : (j + 1) * tail] for j in range(count)]
    return jnp.concatenate([jnp.concatenate(main, axis=0), jnp.concatenate(end, axis=0)], axis=1)


def loop(count, step, group=16):
    group = min(group, count)

    def body(g, carry):
        for u in range(group):
            step(g * group + u)
        return carry

    lax.fori_loop(0, count // group, body, 0)


def condense_kernel(
    elem_in, sharers_in, map_in, inner, inv, couple, face, out, elem, sharers, cmap, rin, invs, cps, fac, sems, small
):
    slots, rhs, width = fac.shape
    step = min(slots, CHUNK)
    chunks = slots // step
    copy = pltpu.make_async_copy

    def part(c):
        return pl.ds(c * step, step)

    def couple_copy(c):
        return copy(couple.at[part(c)], cps.at[part(c)], sems.at[2, c])

    def face_copy(c):
        return copy(face.at[part(c)], fac.at[part(c)], sems.at[3, c])

    first = copy(elem_in, elem, small.at[0])
    others = [copy(sharers_in, sharers, small.at[1]), copy(map_in, cmap, small.at[2])]
    first.start()
    for other in others:
        other.start()
    couple_copy(0).start()
    face_copy(0).start()
    first.wait()
    for c in range(chunks):
        for u in range(step):
            l = c * step + u
            copy(inner.at[elem[0, l]], rin.at[l], sems.at[0, c]).start()
            copy(inv.at[elem[0, l]], invs.at[l], sems.at[1, c]).start()
        if c > 0:
            couple_copy(c).start()
            face_copy(c).start()
    for other in others:
        other.wait()
    maps = cmap[...]
    digits = jnp.concatenate([maps // DIGIT, maps % DIGIT], axis=0).astype(F32)
    local = digits.shape[1]
    spare = LANES - rhs // ROWS * (width - LANES)
    digits = jnp.concatenate([digits, jnp.zeros((ROWS - 2, local), F32)], axis=0)
    extra = jnp.concatenate([jnp.zeros((ROWS, spare - local), F32), digits], axis=1) if spare > local else digits
    for c in range(chunks):
        copy(inner.at[pl.ds(0, step)], rin.at[part(c)], sems.at[0, c]).wait()
        copy(inv.at[pl.ds(0, step)], invs.at[part(c)], sems.at[1, c]).wait()
        near = [dot(rin[c * step + u], invs[c * step + u], NT).astype(BF16) for u in range(step)]
        couple_copy(c).wait()
        face_copy(c).wait()
        for u in range(step):
            l = c * step + u
            value = fac[l].astype(F32) - dot(near[u], cps[l], NT)
            pack(out, l, omega(sharers, l) * value, extra)


def assemble(recv, got, out, sums, rounded):
    slots = got.shape[0]
    rows = sums.shape[1]
    owned = sums.shape[0] - 1
    sums[...] = jnp.zeros_like(sums)

    def add(s):
        j = recv[0, s]
        sums[j] += got[s, :rows].astype(F32)

    loop(slots, add, 32)
    rounded[...] = sums[...].astype(BF16)
    rounded[owned] = jnp.zeros(rounded.shape[1:], BF16)

    def give(s):
        out[s, :rows] = rounded[recv[0, s]]

    loop(slots, give, 32)


def pair_digits(first, d, local):
    last = first.shape[1] - 1
    at = LANES - local
    low = first[d, last].astype(F32)
    top = first[d + 1, last].astype(F32)
    both = jnp.concatenate([low[:2, at:], top[:2, at:]], axis=1).astype(jnp.int32)
    return both[0:1], both[1:2]


def take_lanes(ref, tile, lane):
    rows, total = ref.shape
    lane = jnp.broadcast_to(lane, (rows, LANES))
    tile = jnp.broadcast_to(tile, (rows, LANES))
    taken = None
    for t in range(total // LANES):
        part = jnp.take_along_axis(ref[:, t * LANES : (t + 1) * LANES], lane, axis=1)
        taken = part if taken is None else jnp.where(tile == t, part, taken)
    return taken


def owner_kernel(recv, got, out, sums, rounded):
    assemble(recv, got, out, sums, rounded)


def halves(value, local, left):
    half = value.shape[0] // 2
    top, low = value[:half], value[half:]
    return jnp.where(left, top, pltpu.roll(low, local, 1)), jnp.where(left, pltpu.roll(top, local, 1), low)


def first_owner_kernel(recv, got, cinv, out, sums, rounded, strip):
    slots, height, _, _ = out.shape
    head = got.shape[1]
    piece = strip.shape[0]
    local = LANES // 2
    assemble(recv, got, out, sums, rounded)
    start = pl.multiple_of(lax.axis_index("sub") * piece, piece)
    strip[...] = cinv[pl.ds(start, piece), :]
    left = lax.broadcasted_iota(jnp.int32, (piece // 2, LANES), 1) < local

    def step(p):
        taken = take_lanes(strip, *pair_digits(got, 2 * p, local))
        low, top = halves(taken, local, left)
        for j in range(height - head):
            out[2 * p, head + j] = low[ROWS * j : ROWS * (j + 1)].astype(BF16)
            out[2 * p + 1, head + j] = top[ROWS * j : ROWS * (j + 1)].astype(BF16)

    loop(slots // 2, step)


def restrict_kernel(sharers, got, basis, out, restricted, total):
    slots, rhs, width = restricted.shape
    tail = width - LANES
    group = min(slots, 32)
    total[...] = jnp.zeros_like(total)

    def body(g, carry):
        part = None
        for u in range(group):
            l = g * group + u
            value = (omega(sharers, l) * unpack(got, l, rhs, tail)).astype(BF16)
            restricted[l] = value
            term = dot(value, basis[l], NT)
            part = term if part is None else part + term
        total[...] += part
        return carry

    lax.fori_loop(0, slots // group, body, 0)
    both = total[...]
    block = jnp.concatenate([both[: rhs // 2], both[rhs // 2 :]], axis=1).astype(BF16)

    def give(d):
        out[d] = block

    loop(slots, give, 32)


def turn_columns(groups, rows, got, head, turned):
    local, total = turned.shape
    piece = (got.shape[1] - head) * ROWS * 2
    for t in range(total // LANES):
        parts = []
        for k in range(t * LANES, (t + 1) * LANES, piece):
            device = (k % rows) // piece * groups + k // rows
            block = [got[device, j].astype(F32) for j in range(head, got.shape[1])]
            block = jnp.concatenate(block, axis=0)
            parts += [block, pltpu.roll(block, local, 1)]
        turned[:, t * LANES : (t + 1) * LANES] = jnp.concatenate(parts, axis=0).T[:local]


def correct_kernel(groups, rows, sharers, got, first, second, restricted, inv, basis, out, turned, sums):
    slots, rhs, width = restricted.shape
    head = first.shape[1]
    local = basis.shape[1]
    turn_columns(groups, rows, second, head, turned)
    sums[...] = jnp.zeros_like(sums)
    left = lax.broadcasted_iota(jnp.int32, (rhs // 2, LANES), 1) < local
    group = min(slots // 2, 16)

    def body(g, carry):
        part = None
        for u in range(group):
            p = g * group + u
            columns = take_lanes(turned, *pair_digits(first, 2 * p, local)).astype(BF16)
            low = got[2 * p].astype(F32)
            top = got[2 * p + 1].astype(F32)
            value = jnp.concatenate(halves(jnp.concatenate([low, top], axis=0), local, left), axis=0)
            term = dot(value.astype(BF16), columns, NT)
            part = term if part is None else part + term
        sums[...] += part
        return carry

    lax.fori_loop(0, slots // 2 // group, body, 0)
    picked = sums[...].astype(BF16)
    extra = jnp.zeros((ROWS, LANES - rhs // ROWS * (width - LANES)), F32)

    def finish(l):
        value = dot(picked, basis[l]) + dot(restricted[l], inv[l], NT)
        pack(out, l, omega(sharers, l) * value, extra)

    loop(slots, finish, 32)


def extend_kernel(elem, got, inner, couple, inv, inner_out, face_out, sums, faces, inners, sems):
    slots, rhs, width = faces.shape
    elements = inners.shape[0]
    tail = width - LANES
    sums[...] = inner[...].astype(F32)

    def step(l):
        value = unpack(got, l, rhs, tail).astype(BF16)
        faces[l] = value
        sums[elem[0, l]] -= dot(value, couple[l])

    loop(slots, step, 32)
    copies = [pltpu.make_async_copy(faces, face_out, sems.at[0])]
    copies[0].start()
    part = elements // 2
    for c in range(2):

        def finish(e):
            inners[c * part + e] = dot(sums[c * part + e].astype(BF16), inv[c * part + e], NT).astype(BF16)

        loop(part, finish, 32)
        span = pl.ds(c * part, part)
        copies.append(pltpu.make_async_copy(inners.at[span], inner_out.at[span], sems.at[1 + c]))
        copies[-1].start()
    for each in copies:
        each.wait()


def padded(shape, dtype):
    size = jnp.dtype(dtype).itemsize
    for n in shape[:-2]:
        size *= n
    high = shape[-2] if shape[-2] < 8 else -(-shape[-2] // 16) * 16
    return size * high * (-(-shape[-1] // LANES) * LANES)


def call(kernel, out_shape, specs, args, scratch=(), flops=0, name=None, limit=None, out_spec=VMEM):
    many = isinstance(out_shape, (tuple, list))
    outs = tuple(out_shape) if many else (out_shape,)
    held = [a for a, s in zip(args, specs) if s is VMEM] + list(outs)
    need = sum(padded(a.shape, a.dtype) for a in held)
    room = sum(padded(shape, dtype) for shape, dtype in scratch if dtype is not None)
    made = [pltpu.VMEM(shape, dtype) if dtype is not None else shape for shape, dtype in scratch]
    return pl.pallas_call(
        kernel,
        out_shape=out_shape,
        in_specs=specs,
        out_specs=tuple(out_spec for _ in outs) if many else out_spec,
        scratch_shapes=made,
        cost_estimate=pl.CostEstimate(flops=flops, bytes_accessed=need, transcendentals=0),
        compiler_params=pltpu.CompilerParams(vmem_limit_bytes=limit or need + room + (2 << 20)),
        name=name,
    )(*args)


def body(
    res_inner,
    res_face,
    inner_inv,
    face_coupling,
    face_elem,
    face_inv,
    coarse_basis,
    coarse_map,
    coarse_inv,
    recv_index,
    sharers,
):
    slots, rhs, width = res_face.shape
    owned = slots // 4
    elements = res_inner.shape[0]
    rows, total = coarse_inv.shape
    local = coarse_map.shape[1]
    groups = total // rows
    piece = rows * groups // slots
    shape = jax.ShapeDtypeStruct
    head = rhs // ROWS + 1
    wire = shape((slots, head, ROWS, LANES), BF16)
    unit = 2 * rhs * width * width
    tables = [((owned + 1, head, ROWS, LANES), F32), ((owned + 1, head, ROWS, LANES), BF16)]

    sent = call(
        condense_kernel,
        wire,
        [HBM] * 7,
        tuple(
            pltpu.with_memory_space_constraint(x, pltpu.HBM)
            for x in (face_elem, sharers, coarse_map, res_inner, inner_inv, face_coupling, res_face)
        ),
        [
            (pltpu.SMEM(face_elem.shape, jnp.int32), None),
            (pltpu.SMEM(sharers.shape, jnp.int32), None),
            (pltpu.VMEM(coarse_map.shape, jnp.int32), None),
            ((slots, rhs, width), BF16),
            ((slots, width, width), BF16),
            ((slots, width, width), BF16),
            ((slots, rhs, width), BF16),
            (pltpu.SemaphoreType.DMA((4, -(-slots // CHUNK))), None),
            (pltpu.SemaphoreType.DMA((3,)), None),
        ],
        flops=2 * slots * unit,
        name="condense",
    )
    first = exchange(sent)
    held = call(
        first_owner_kernel,
        shape((slots, head + piece // (2 * ROWS), ROWS, LANES), BF16),
        [SMEM, VMEM, VMEM],
        (recv_index, first, coarse_inv),
        tables + [((piece, total), F32)],
        flops=100 * slots * unit,
        name="first_owner",
    )
    gathered = exchange(held)
    coarse, restricted = call(
        restrict_kernel,
        (shape((slots, rhs // 2, LANES), BF16), shape((slots, rhs, width), BF16)),
        [SMEM, VMEM, VMEM],
        (sharers, gathered, coarse_basis),
        [((rhs, local), F32)],
        flops=100 * slots * unit,
        name="restrict",
    )
    every = exchange(coarse)
    weighted = call(
        functools.partial(correct_kernel, groups, rows),
        wire,
        [SMEM, VMEM, VMEM, VMEM, VMEM, VMEM, VMEM],
        (sharers, every, first, gathered, restricted, face_inv, coarse_basis),
        [((local, total), F32), ((rhs, local), F32)],
        flops=2 * slots * unit,
        name="correct",
    )
    third = exchange(weighted)
    spread = call(
        owner_kernel, wire, [SMEM, VMEM], (recv_index, third), tables, flops=slots * width * LANES, name="owner"
    )
    assembled = exchange(spread)
    return call(
        extend_kernel,
        (shape((elements, rhs, width), BF16), shape((slots, rhs, width), BF16)),
        [SMEM, VMEM, VMEM, VMEM, VMEM],
        (face_elem, assembled, res_inner, face_coupling, inner_inv),
        [
            ((elements, rhs, width), F32),
            ((slots, rhs, width), BF16),
            ((elements, rhs, width), BF16),
            (pltpu.SemaphoreType.DMA((3,)), None),
        ],
        flops=2 * slots * unit,
        name="extend",
        out_spec=HBM,
    )


def solution(mesh):
    block = P(AXES, None, None)
    row = P(AXES, None)
    return jax.shard_map(
        body,
        mesh=mesh,
        in_specs=(block, block, block, block, row, block, block, row, P("grp", None), row, row),
        out_specs=(block, block),
        check_vma=False,
    )
```

```python
import functools

import jax
import jax.numpy as jnp
from jax import lax
from jax.experimental import pallas as pl
from jax.experimental.pallas import tpu as pltpu
from jax.sharding import PartitionSpec as P

AXES = ("sub", "grp")
DIGIT = 128
LANES = 128
NT = (((1,), (1,)), ((), ()))
NN = (((1,), (0,)), ((), ()))
F32 = jnp.float32
BF16 = jnp.bfloat16
VMEM = pl.BlockSpec(memory_space=pltpu.VMEM)
HBM = pl.BlockSpec(memory_space=pltpu.HBM)
CHUNK = 16
ROWS = 4
GROUP = 32


def exchange(blocks):
    return lax.all_to_all(blocks, AXES, split_axis=0, concat_axis=0, tiled=True)


def dot(a, b, dims=NN):
    return lax.dot_general(a, b, dims, preferred_element_type=F32)


def omega(sharers, slot):
    count = sharers[0, slot]
    return jnp.where(count > 0, 1.0 / jnp.maximum(count, 1).astype(F32), 0.0)


def pack(out, slot, value, extra):
    count = value.shape[0] // ROWS
    value_rows = [value[ROWS * j : ROWS * (j + 1)] for j in range(count)]
    for j in range(count):
        out[slot, j] = value_rows[j][:, :LANES].astype(BF16)
    out[slot, count] = jnp.concatenate([v[:, LANES:] for v in value_rows] + [extra], axis=1).astype(BF16)


def unpack(ref, slot, rhs, tail):
    count = rhs // ROWS
    main = [ref[slot, j].astype(F32) for j in range(count)]
    last = ref[slot, count].astype(F32)
    end = [last[:, j * tail : (j + 1) * tail] for j in range(count)]
    return jnp.concatenate([jnp.concatenate(main, axis=0), jnp.concatenate(end, axis=0)], axis=1)


def loop(count, step, group=16):
    group = min(group, count)

    def body(g, carry):
        for u in range(group):
            step(g * group + u)
        return carry

    lax.fori_loop(0, count // group, body, 0)


def table_loop(table, step):
    rows, group = table.shape

    def body(g, carry):
        row = table[pl.ds(g, 1), :]
        for u in range(group):
            step(g * group + u, row[0, u])
        return carry

    lax.fori_loop(0, rows, body, 0)


def weights(sharers, g):
    count = sharers[pl.ds(g, 1), :]
    return jnp.where(count > 0, 1.0 / jnp.maximum(count, 1).astype(F32), 0.0)


def condense_kernel(
    elem_in, sharers_in, map_in, inner, inv, couple, face, out, elem, sharers, cmap, rin, invs, cps, fac, sems, small
):
    slots, rhs, width = fac.shape
    step = min(slots, CHUNK)
    chunks = slots // step
    copy = pltpu.make_async_copy

    def part(c):
        return pl.ds(c * step, step)

    def couple_copy(c):
        return copy(couple.at[part(c)], cps.at[part(c)], sems.at[2, c])

    def face_copy(c):
        return copy(face.at[part(c)], fac.at[part(c)], sems.at[3, c])

    first = copy(elem_in, elem, small.at[0])
    others = [copy(sharers_in, sharers, small.at[1]), copy(map_in, cmap, small.at[2])]
    first.start()
    for other in others:
        other.start()
    couple_copy(0).start()
    face_copy(0).start()
    first.wait()
    for c in range(chunks):
        for u in range(step):
            l = c * step + u
            copy(inner.at[elem[0, l]], rin.at[l], sems.at[0, c]).start()
            copy(inv.at[elem[0, l]], invs.at[l], sems.at[1, c]).start()
        if c > 0:
            couple_copy(c).start()
            face_copy(c).start()
    for other in others:
        other.wait()
    maps = cmap[...]
    digits = jnp.concatenate([maps // DIGIT, maps % DIGIT], axis=0).astype(F32)
    local = digits.shape[1]
    spare = LANES - rhs // ROWS * (width - LANES)
    digits = jnp.concatenate([digits, jnp.zeros((ROWS - 2, local), F32)], axis=0)
    extra = jnp.concatenate([jnp.zeros((ROWS, spare - local), F32), digits], axis=1) if spare > local else digits
    for c in range(chunks):
        copy(inner.at[pl.ds(0, step)], rin.at[part(c)], sems.at[0, c]).wait()
        copy(inv.at[pl.ds(0, step)], invs.at[part(c)], sems.at[1, c]).wait()
        near = [dot(rin[c * step + u], invs[c * step + u], NT).astype(BF16) for u in range(step)]
        couple_copy(c).wait()
        face_copy(c).wait()
        for u in range(step):
            l = c * step + u
            value = fac[l].astype(F32) - dot(near[u], cps[l], NT)
            pack(out, l, omega(sharers, l) * value, extra)


def assemble(recv, got, out, sums, rounded):
    rows = sums.shape[1]
    owned = sums.shape[0] - 1
    sums[...] = jnp.zeros_like(sums)

    def add(s, j):
        sums[j] += got[s, :rows].astype(F32)

    table_loop(recv, add)
    rounded[...] = sums[...].astype(BF16)
    rounded[owned] = jnp.zeros(rounded.shape[1:], BF16)

    def give(s, j):
        out[s, :rows] = rounded[j]

    table_loop(recv, give)


def pair_digits(first, d, local):
    last = first.shape[1] - 1
    at = LANES - local
    low = first[d, last].astype(F32)
    top = first[d + 1, last].astype(F32)
    both = jnp.concatenate([low[:2, at:], top[:2, at:]], axis=1).astype(jnp.int32)
    return both[0:1], both[1:2]


def take_lanes(ref, tile, lane):
    rows, total = ref.shape
    lane = jnp.broadcast_to(lane, (rows, LANES))
    tile = jnp.broadcast_to(tile, (rows, LANES))
    taken = None
    for t in range(total // LANES):
        part = jnp.take_along_axis(ref[:, t * LANES : (t + 1) * LANES], lane, axis=1)
        taken = part if taken is None else jnp.where(tile == t, part, taken)
    return taken


def owner_kernel(recv, got, out, sums, rounded):
    assemble(recv, got, out, sums, rounded)


def halves(value, local, left):
    half = value.shape[0] // 2
    top, low = value[:half], value[half:]
    return jnp.where(left, top, pltpu.roll(low, local, 1)), jnp.where(left, pltpu.roll(top, local, 1), low)


def first_owner_kernel(recv, got, cinv, out, sums, rounded, strip):
    slots, height, _, _ = out.shape
    head = got.shape[1]
    piece = strip.shape[0]
    local = LANES // 2
    start = pl.multiple_of(lax.axis_index("sub") * piece, piece)
    strip[...] = cinv[pl.ds(start, piece), :]
    left = lax.broadcasted_iota(jnp.int32, (piece // 2, LANES), 1) < local

    def step(p):
        taken = take_lanes(strip, *pair_digits(got, 2 * p, local))
        low, top = halves(taken, local, left)
        for j in range(height - head):
            out[2 * p, head + j] = low[ROWS * j : ROWS * (j + 1)].astype(BF16)
            out[2 * p + 1, head + j] = top[ROWS * j : ROWS * (j + 1)].astype(BF16)

    loop(slots // 2, step)
    assemble(recv, got, out, sums, rounded)


def restrict_kernel(sharers, got, basis, out, restricted, total):
    slots, rhs, width = restricted.shape
    tail = width - LANES
    groups, group = sharers.shape
    total[...] = jnp.zeros_like(total)

    def body(g, carry):
        part = None
        weight = weights(sharers, g)
        for u in range(group):
            l = g * group + u
            value = (weight[:, u : u + 1] * unpack(got, l, rhs, tail)).astype(BF16)
            restricted[l] = value
            term = dot(value, basis[l], NT)
            part = term if part is None else part + term
        total[...] += part
        return carry

    lax.fori_loop(0, groups, body, 0)
    both = total[...]
    block = jnp.concatenate([both[: rhs // 2], both[rhs // 2 :]], axis=1).astype(BF16)

    def give(d):
        out[d] = block

    loop(slots, give, 32)


def turn_columns(groups, rows, got, head, turned):
    local, total = turned.shape
    piece = (got.shape[1] - head) * ROWS * 2
    for t in range(total // LANES):
        parts = []
        for k in range(t * LANES, (t + 1) * LANES, piece):
            device = (k % rows) // piece * groups + k // rows
            block = [got[device, j].astype(F32) for j in range(head, got.shape[1])]
            block = jnp.concatenate(block, axis=0)
            parts += [block, pltpu.roll(block, local, 1)]
        turned[:, t * LANES : (t + 1) * LANES] = jnp.concatenate(parts, axis=0).T[:local]


def correct_kernel(groups, rows, sharers, got, first, second, restricted, inv, basis, out, turned, sums):
    slots, rhs, width = restricted.shape
    head = first.shape[1]
    local = basis.shape[1]
    turn_columns(groups, rows, second, head, turned)
    sums[...] = jnp.zeros_like(sums)
    left = lax.broadcasted_iota(jnp.int32, (rhs // 2, LANES), 1) < local
    group = min(slots // 2, 16)

    def body(g, carry):
        part = None
        for u in range(group):
            p = g * group + u
            columns = take_lanes(turned, *pair_digits(first, 2 * p, local)).astype(BF16)
            low = got[2 * p].astype(F32)
            top = got[2 * p + 1].astype(F32)
            value = jnp.concatenate(halves(jnp.concatenate([low, top], axis=0), local, left), axis=0)
            term = dot(value.astype(BF16), columns, NT)
            part = term if part is None else part + term
        sums[...] += part
        return carry

    lax.fori_loop(0, slots // 2 // group, body, 0)
    picked = sums[...].astype(BF16)
    extra = jnp.zeros((ROWS, LANES - rhs // ROWS * (width - LANES)), F32)

    def finish(g, carry):
        weight = weights(sharers, g)
        for u in range(sharers.shape[1]):
            l = g * sharers.shape[1] + u
            value = dot(picked, basis[l]) + dot(restricted[l], inv[l], NT)
            pack(out, l, weight[:, u : u + 1] * value, extra)
        return carry

    lax.fori_loop(0, sharers.shape[0], finish, 0)


def extend_kernel(elem, got, inner, couple, inv, inner_out, face_out, sums, faces, inners, sems):
    slots, rhs, width = faces.shape
    elements = inners.shape[0]
    tail = width - LANES
    sums[...] = inner[...].astype(F32)

    def step(l, e):
        value = unpack(got, l, rhs, tail).astype(BF16)
        faces[l] = value
        sums[e] -= dot(value, couple[l])

    table_loop(elem, step)
    copies = [pltpu.make_async_copy(faces, face_out, sems.at[0])]
    copies[0].start()
    part = elements // 2
    for c in range(2):

        def finish(e):
            inners[c * part + e] = dot(sums[c * part + e].astype(BF16), inv[c * part + e], NT).astype(BF16)

        loop(part, finish, 32)
        span = pl.ds(c * part, part)
        copies.append(pltpu.make_async_copy(inners.at[span], inner_out.at[span], sems.at[1 + c]))
        copies[-1].start()
    for each in copies:
        each.wait()


def padded(shape, dtype):
    size = jnp.dtype(dtype).itemsize
    for n in shape[:-2]:
        size *= n
    high = shape[-2] if shape[-2] < 8 else -(-shape[-2] // 16) * 16
    return size * high * (-(-shape[-1] // LANES) * LANES)


def call(kernel, out_shape, specs, args, scratch=(), flops=0, name=None, limit=None, out_spec=VMEM):
    many = isinstance(out_shape, (tuple, list))
    outs = tuple(out_shape) if many else (out_shape,)
    held = [a for a, s in zip(args, specs) if s is VMEM] + list(outs)
    need = sum(padded(a.shape, a.dtype) for a in held)
    room = sum(padded(shape, dtype) for shape, dtype in scratch if dtype is not None)
    made = [pltpu.VMEM(shape, dtype) if dtype is not None else shape for shape, dtype in scratch]
    return pl.pallas_call(
        kernel,
        out_shape=out_shape,
        in_specs=specs,
        out_specs=tuple(out_spec for _ in outs) if many else out_spec,
        scratch_shapes=made,
        cost_estimate=pl.CostEstimate(flops=flops, bytes_accessed=need, transcendentals=0),
        compiler_params=pltpu.CompilerParams(vmem_limit_bytes=limit or need + room + (2 << 20)),
        name=name,
    )(*args)


def body(
    res_inner,
    res_face,
    inner_inv,
    face_coupling,
    face_elem,
    face_inv,
    coarse_basis,
    coarse_map,
    coarse_inv,
    recv_index,
    sharers,
):
    slots, rhs, width = res_face.shape
    owned = slots // 4
    elements = res_inner.shape[0]
    rows, total = coarse_inv.shape
    local = coarse_map.shape[1]
    groups = total // rows
    piece = rows * groups // slots
    shape = jax.ShapeDtypeStruct
    head = rhs // ROWS + 1
    wire = shape((slots, head, ROWS, LANES), BF16)
    unit = 2 * rhs * width * width
    recv_table, sharers_table, elem_table = (
        x.reshape(-1, min(slots, GROUP)) for x in (recv_index, sharers, face_elem)
    )
    tables = [((owned + 1, head, ROWS, LANES), F32), ((owned + 1, head, ROWS, LANES), BF16)]

    sent = call(
        condense_kernel,
        wire,
        [HBM] * 7,
        tuple(
            pltpu.with_memory_space_constraint(x, pltpu.HBM)
            for x in (face_elem, sharers, coarse_map, res_inner, inner_inv, face_coupling, res_face)
        ),
        [
            (pltpu.SMEM(face_elem.shape, jnp.int32), None),
            (pltpu.SMEM(sharers.shape, jnp.int32), None),
            (pltpu.VMEM(coarse_map.shape, jnp.int32), None),
            ((slots, rhs, width), BF16),
            ((slots, width, width), BF16),
            ((slots, width, width), BF16),
            ((slots, rhs, width), BF16),
            (pltpu.SemaphoreType.DMA((4, -(-slots // CHUNK))), None),
            (pltpu.SemaphoreType.DMA((3,)), None),
        ],
        flops=2 * slots * unit,
        name="condense",
    )
    first = exchange(sent)
    held = call(
        first_owner_kernel,
        shape((slots, head + piece // (2 * ROWS), ROWS, LANES), BF16),
        [VMEM, VMEM, VMEM],
        (recv_table, first, coarse_inv),
        tables + [((piece, total), F32)],
        flops=100 * slots * unit,
        name="first_owner",
    )
    gathered = exchange(held)
    coarse, restricted = call(
        restrict_kernel,
        (shape((slots, rhs // 2, LANES), BF16), shape((slots, rhs, width), BF16)),
        [VMEM, VMEM, VMEM],
        (sharers_table, gathered, coarse_basis),
        [((rhs, local), F32)],
        flops=100 * slots * unit,
        name="restrict",
    )
    every = exchange(coarse)
    weighted = call(
        functools.partial(correct_kernel, groups, rows),
        wire,
        [VMEM] * 7,
        (sharers_table, every, first, gathered, restricted, face_inv, coarse_basis),
        [((local, total), F32), ((rhs, local), F32)],
        flops=2 * slots * unit,
        name="correct",
    )
    third = exchange(weighted)
    spread = call(
        owner_kernel, wire, [VMEM, VMEM], (recv_table, third), tables, flops=slots * width * LANES, name="owner"
    )
    assembled = exchange(spread)
    return call(
        extend_kernel,
        (shape((elements, rhs, width), BF16), shape((slots, rhs, width), BF16)),
        [VMEM] * 5,
        (elem_table, assembled, res_inner, face_coupling, inner_inv),
        [
            ((elements, rhs, width), F32),
            ((slots, rhs, width), BF16),
            ((elements, rhs, width), BF16),
            (pltpu.SemaphoreType.DMA((3,)), None),
        ],
        flops=2 * slots * unit,
        name="extend",
        out_spec=HBM,
    )


def solution(mesh):
    block = P(AXES, None, None)
    row = P(AXES, None)
    return jax.shard_map(
        body,
        mesh=mesh,
        in_specs=(block, block, block, block, row, block, block, row, P("grp", None), row, row),
        out_specs=(block, block),
        check_vma=False,
    )
```

```python
import functools

import jax
import jax.numpy as jnp
from jax import lax
from jax.experimental import pallas as pl
from jax.experimental.pallas import tpu as pltpu
from jax.sharding import PartitionSpec as P

AXES = ("sub", "grp")
DIGIT = 128
LANES = 128
NT = (((1,), (1,)), ((), ()))
NN = (((1,), (0,)), ((), ()))
F32 = jnp.float32
BF16 = jnp.bfloat16
VMEM = pl.BlockSpec(memory_space=pltpu.VMEM)
HBM = pl.BlockSpec(memory_space=pltpu.HBM)
CHUNK = 16
ROWS = 2
GROUP = 32


def exchange(blocks):
    return lax.all_to_all(blocks, AXES, split_axis=0, concat_axis=0, tiled=True)


def dot(a, b, dims=NN):
    return lax.dot_general(a, b, dims, preferred_element_type=F32)


def omega(sharers, slot):
    count = sharers[0, slot]
    return jnp.where(count > 0, 1.0 / jnp.maximum(count, 1).astype(F32), 0.0)


def pack(out, slot, value):
    count = value.shape[0] // ROWS
    value_rows = [value[ROWS * j : ROWS * (j + 1)] for j in range(count)]
    for j in range(count):
        out[slot, j] = value_rows[j][:, :LANES].astype(BF16)
    out[slot, count] = jnp.concatenate([v[:, LANES:] for v in value_rows], axis=1).astype(BF16)


def unpack(ref, slot, rhs, tail):
    count = rhs // ROWS
    main = [ref[slot, j].astype(F32) for j in range(count)]
    last = ref[slot, count].astype(F32)
    end = [last[:, j * tail : (j + 1) * tail] for j in range(count)]
    return jnp.concatenate([jnp.concatenate(main, axis=0), jnp.concatenate(end, axis=0)], axis=1)


def loop(count, step, group=16):
    group = min(group, count)

    def body(g, carry):
        for u in range(group):
            step(g * group + u)
        return carry

    lax.fori_loop(0, count // group, body, 0)


def table_loop(table, step):
    rows, group = table.shape

    def body(g, carry):
        row = table[pl.ds(g, 1), :]
        for u in range(group):
            step(g * group + u, row[0, u])
        return carry

    lax.fori_loop(0, rows, body, 0)


def weights(sharers, g):
    count = sharers[pl.ds(g, 1), :]
    return jnp.where(count > 0, 1.0 / jnp.maximum(count, 1).astype(F32), 0.0)


def condense_kernel(
    elem_in, sharers_in, map_in, inner, inv, couple, face, out, elem, sharers, cmap, rin, invs, cps, fac, sems, small
):
    slots, rhs, width = fac.shape
    step = min(slots, CHUNK)
    chunks = slots // step
    copy = pltpu.make_async_copy

    def part(c):
        return pl.ds(c * step, step)

    def couple_copy(c):
        return copy(couple.at[part(c)], cps.at[part(c)], sems.at[2, c])

    def face_copy(c):
        return copy(face.at[part(c)], fac.at[part(c)], sems.at[3, c])

    first = copy(elem_in, elem, small.at[0])
    others = [copy(sharers_in, sharers, small.at[1]), copy(map_in, cmap, small.at[2])]
    first.start()
    for other in others:
        other.start()
    couple_copy(0).start()
    face_copy(0).start()
    first.wait()
    for c in range(chunks):
        for u in range(step):
            l = c * step + u
            copy(inner.at[elem[0, l]], rin.at[l], sems.at[0, c]).start()
            copy(inv.at[elem[0, l]], invs.at[l], sems.at[1, c]).start()
        if c > 0:
            couple_copy(c).start()
            face_copy(c).start()
    for other in others:
        other.wait()
    maps = cmap[...]
    digits = jnp.concatenate([maps // DIGIT, maps % DIGIT], axis=0).astype(F32)
    local = digits.shape[1]
    digits = jnp.concatenate([jnp.zeros((ROWS, LANES - local), F32), digits], axis=1).astype(BF16)
    last = out.shape[1] - 1
    for c in range(chunks):
        copy(inner.at[pl.ds(0, step)], rin.at[part(c)], sems.at[0, c]).wait()
        copy(inv.at[pl.ds(0, step)], invs.at[part(c)], sems.at[1, c]).wait()
        near = [dot(rin[c * step + u], invs[c * step + u], NT).astype(BF16) for u in range(step)]
        couple_copy(c).wait()
        face_copy(c).wait()
        for u in range(step):
            l = c * step + u
            value = fac[l].astype(F32) - dot(near[u], cps[l], NT)
            pack(out, l, omega(sharers, l) * value)
            out[l, last] = digits


def assemble(recv, got, out, sums, rounded):
    rows = sums.shape[1]
    owned = sums.shape[0] - 1
    sums[...] = jnp.zeros_like(sums)

    def add(s, j):
        sums[j] += got[s, :rows].astype(F32)

    table_loop(recv, add)
    rounded[...] = sums[...].astype(BF16)
    rounded[owned] = jnp.zeros(rounded.shape[1:], BF16)

    def give(s, j):
        out[s, :rows] = rounded[j]

    table_loop(recv, give)


def pair_digits(first, d, local):
    last = first.shape[1] - 1
    at = LANES - local
    low = first[d, last].astype(F32)
    top = first[d + 1, last].astype(F32)
    both = jnp.concatenate([low[:2, at:], top[:2, at:]], axis=1).astype(jnp.int32)
    return both[0:1], both[1:2]


def take_lanes(ref, tile, lane):
    rows, total = ref.shape
    lane = jnp.broadcast_to(lane, (rows, LANES))
    tile = jnp.broadcast_to(tile, (rows, LANES))
    taken = None
    for t in range(total // LANES):
        part = jnp.take_along_axis(ref[:, t * LANES : (t + 1) * LANES], lane, axis=1)
        taken = part if taken is None else jnp.where(tile == t, part, taken)
    return taken


def owner_kernel(recv, got, out, sums, rounded):
    assemble(recv, got, out, sums, rounded)


def halves(value, local, left):
    half = value.shape[0] // 2
    top, low = value[:half], value[half:]
    return jnp.where(left, top, pltpu.roll(low, local, 1)), jnp.where(left, pltpu.roll(top, local, 1), low)


def first_owner_kernel(recv, got, cinv, out, sums, rounded, strip):
    slots, height, _, _ = out.shape
    head = sums.shape[1]
    piece = strip.shape[0]
    local = LANES // 2
    start = pl.multiple_of(lax.axis_index("sub") * piece, piece)
    strip[...] = cinv[pl.ds(start, piece), :]
    left = lax.broadcasted_iota(jnp.int32, (piece // 2, LANES), 1) < local

    def step(p):
        taken = take_lanes(strip, *pair_digits(got, 2 * p, local))
        low, top = halves(taken, local, left)
        for j in range(height - head):
            out[2 * p, head + j] = low[ROWS * j : ROWS * (j + 1)].astype(BF16)
            out[2 * p + 1, head + j] = top[ROWS * j : ROWS * (j + 1)].astype(BF16)

    loop(slots // 2, step)
    assemble(recv, got, out, sums, rounded)


def restrict_kernel(sharers, got, basis, out, restricted, total):
    slots, rhs, width = restricted.shape
    tail = width - LANES
    groups, group = sharers.shape
    total[...] = jnp.zeros_like(total)

    def body(g, carry):
        part = None
        weight = weights(sharers, g)
        for u in range(group):
            l = g * group + u
            value = (weight[:, u : u + 1] * unpack(got, l, rhs, tail)).astype(BF16)
            restricted[l] = value
            term = dot(value, basis[l], NT)
            part = term if part is None else part + term
        total[...] += part
        return carry

    lax.fori_loop(0, groups, body, 0)
    both = total[...]
    block = jnp.concatenate([both[: rhs // 2], both[rhs // 2 :]], axis=1).astype(BF16)

    def give(d):
        out[d] = block

    loop(slots, give, 32)


def turn_columns(groups, rows, got, head, turned):
    local, total = turned.shape
    piece = (got.shape[1] - head) * ROWS * 2
    for t in range(total // LANES):
        parts = []
        for k in range(t * LANES, (t + 1) * LANES, piece):
            device = (k % rows) // piece * groups + k // rows
            block = [got[device, j].astype(F32) for j in range(head, got.shape[1])]
            block = jnp.concatenate(block, axis=0)
            parts += [block, pltpu.roll(block, local, 1)]
        turned[:, t * LANES : (t + 1) * LANES] = jnp.concatenate(parts, axis=0).T[:local]


def correct_kernel(groups, rows, sharers, got, first, second, restricted, inv, basis, out, turned, sums, near):
    slots, rhs, width = restricted.shape
    head = first.shape[1] - 1
    local = basis.shape[1]
    turn_columns(groups, rows, second, head, turned)
    sums[...] = jnp.zeros_like(sums)
    left = lax.broadcasted_iota(jnp.int32, (rhs // 2, LANES), 1) < local
    group = min(slots // 2, 16)

    def body(g, carry):
        part = None
        for u in range(group):
            p = g * group + u
            columns = take_lanes(turned, *pair_digits(first, 2 * p, local)).astype(BF16)
            low = got[2 * p].astype(F32)
            top = got[2 * p + 1].astype(F32)
            value = jnp.concatenate(halves(jnp.concatenate([low, top], axis=0), local, left), axis=0)
            term = dot(value.astype(BF16), columns, NT)
            part = term if part is None else part + term
            for l in (2 * p, 2 * p + 1):
                near[l] = dot(restricted[l], inv[l], NT)
        sums[...] += part
        return carry

    lax.fori_loop(0, slots // 2 // group, body, 0)
    picked = sums[...].astype(BF16)
    def finish(g, carry):
        weight = weights(sharers, g)
        for u in range(sharers.shape[1]):
            l = g * sharers.shape[1] + u
            value = dot(picked, basis[l]) + near[l]
            pack(out, l, weight[:, u : u + 1] * value)
        return carry

    lax.fori_loop(0, sharers.shape[0], finish, 0)


def extend_kernel(elem, got, inner, couple, inv, inner_out, face_out, sums, faces, inners, sems):
    slots, rhs, width = faces.shape
    elements = inners.shape[0]
    tail = width - LANES
    sums[...] = inner[...].astype(F32)

    def step(l, e):
        value = unpack(got, l, rhs, tail).astype(BF16)
        faces[l] = value
        sums[e] -= dot(value, couple[l])

    table_loop(elem, step)
    copies = [pltpu.make_async_copy(faces, face_out, sems.at[0])]
    copies[0].start()
    part = elements // 2
    for c in range(2):

        def finish(e):
            inners[c * part + e] = dot(sums[c * part + e].astype(BF16), inv[c * part + e], NT).astype(BF16)

        loop(part, finish, 32)
        span = pl.ds(c * part, part)
        copies.append(pltpu.make_async_copy(inners.at[span], inner_out.at[span], sems.at[1 + c]))
        copies[-1].start()
    for each in copies:
        each.wait()


def padded(shape, dtype):
    size = jnp.dtype(dtype).itemsize
    for n in shape[:-2]:
        size *= n
    high = shape[-2] if shape[-2] < 8 else -(-shape[-2] // 16) * 16
    return size * high * (-(-shape[-1] // LANES) * LANES)


def call(kernel, out_shape, specs, args, scratch=(), flops=0, name=None, limit=None, out_spec=VMEM):
    many = isinstance(out_shape, (tuple, list))
    outs = tuple(out_shape) if many else (out_shape,)
    held = [a for a, s in zip(args, specs) if s is VMEM] + list(outs)
    need = sum(padded(a.shape, a.dtype) for a in held)
    room = sum(padded(shape, dtype) for shape, dtype in scratch if dtype is not None)
    made = [pltpu.VMEM(shape, dtype) if dtype is not None else shape for shape, dtype in scratch]
    return pl.pallas_call(
        kernel,
        out_shape=out_shape,
        in_specs=specs,
        out_specs=tuple(out_spec for _ in outs) if many else out_spec,
        scratch_shapes=made,
        cost_estimate=pl.CostEstimate(flops=flops, bytes_accessed=need, transcendentals=0),
        compiler_params=pltpu.CompilerParams(vmem_limit_bytes=limit or need + room + (2 << 20)),
        name=name,
    )(*args)


def body(
    res_inner,
    res_face,
    inner_inv,
    face_coupling,
    face_elem,
    face_inv,
    coarse_basis,
    coarse_map,
    coarse_inv,
    recv_index,
    sharers,
):
    slots, rhs, width = res_face.shape
    owned = slots // 4
    elements = res_inner.shape[0]
    rows, total = coarse_inv.shape
    local = coarse_map.shape[1]
    groups = total // rows
    piece = rows * groups // slots
    shape = jax.ShapeDtypeStruct
    head = rhs // ROWS + 1
    wire = shape((slots, head, ROWS, LANES), BF16)
    unit = 2 * rhs * width * width
    recv_table, sharers_table, elem_table = (
        x.reshape(-1, min(slots, GROUP)) for x in (recv_index, sharers, face_elem)
    )
    tables = [((owned + 1, head, ROWS, LANES), F32), ((owned + 1, head, ROWS, LANES), BF16)]

    sent = call(
        condense_kernel,
        shape((slots, head + 1, ROWS, LANES), BF16),
        [HBM] * 7,
        tuple(
            pltpu.with_memory_space_constraint(x, pltpu.HBM)
            for x in (face_elem, sharers, coarse_map, res_inner, inner_inv, face_coupling, res_face)
        ),
        [
            (pltpu.SMEM(face_elem.shape, jnp.int32), None),
            (pltpu.SMEM(sharers.shape, jnp.int32), None),
            (pltpu.VMEM(coarse_map.shape, jnp.int32), None),
            ((slots, rhs, width), BF16),
            ((slots, width, width), BF16),
            ((slots, width, width), BF16),
            ((slots, rhs, width), BF16),
            (pltpu.SemaphoreType.DMA((4, -(-slots // CHUNK))), None),
            (pltpu.SemaphoreType.DMA((3,)), None),
        ],
        flops=2 * slots * unit,
        name="condense",
    )
    first = exchange(sent)
    held = call(
        first_owner_kernel,
        shape((slots, head + piece // (2 * ROWS), ROWS, LANES), BF16),
        [VMEM, VMEM, VMEM],
        (recv_table, first, coarse_inv),
        tables + [((piece, total), F32)],
        flops=100 * slots * unit,
        name="first_owner",
    )
    gathered = exchange(held)
    coarse, restricted = call(
        restrict_kernel,
        (shape((slots, rhs // 2, LANES), BF16), shape((slots, rhs, width), BF16)),
        [VMEM, VMEM, VMEM],
        (sharers_table, gathered, coarse_basis),
        [((rhs, local), F32)],
        flops=100 * slots * unit,
        name="restrict",
    )
    every = exchange(coarse)
    weighted = call(
        functools.partial(correct_kernel, groups, rows),
        wire,
        [VMEM] * 7,
        (sharers_table, every, first, gathered, restricted, face_inv, coarse_basis),
        [((local, total), F32), ((rhs, local), F32), ((slots, rhs, width), F32)],
        flops=2 * slots * unit,
        name="correct",
    )
    third = exchange(weighted)
    spread = call(
        owner_kernel, wire, [VMEM, VMEM], (recv_table, third), tables, flops=slots * width * LANES, name="owner"
    )
    assembled = exchange(spread)
    return call(
        extend_kernel,
        (shape((elements, rhs, width), BF16), shape((slots, rhs, width), BF16)),
        [VMEM] * 5,
        (elem_table, assembled, res_inner, face_coupling, inner_inv),
        [
            ((elements, rhs, width), F32),
            ((slots, rhs, width), BF16),
            ((elements, rhs, width), BF16),
            (pltpu.SemaphoreType.DMA((3,)), None),
        ],
        flops=2 * slots * unit,
        name="extend",
        out_spec=HBM,
    )


def solution(mesh):
    block = P(AXES, None, None)
    row = P(AXES, None)
    return jax.shard_map(
        body,
        mesh=mesh,
        in_specs=(block, block, block, block, row, block, block, row, P("grp", None), row, row),
        out_specs=(block, block),
        check_vma=False,
    )
```

```python
import functools

import jax
import jax.numpy as jnp
from jax import lax
from jax.experimental import pallas as pl
from jax.experimental.pallas import tpu as pltpu
from jax.sharding import PartitionSpec as P

AXES = ("sub", "grp")
DIGIT = 128
LANES = 128
NT = (((1,), (1,)), ((), ()))
NN = (((1,), (0,)), ((), ()))
F32 = jnp.float32
BF16 = jnp.bfloat16
VMEM = pl.BlockSpec(memory_space=pltpu.VMEM)
HBM = pl.BlockSpec(memory_space=pltpu.HBM)
CHUNK = 16
ROWS = 2
GROUP = 32


def exchange(blocks):
    return lax.all_to_all(blocks, AXES, split_axis=0, concat_axis=0, tiled=True)


def dot(a, b, dims=NN):
    return lax.dot_general(a, b, dims, preferred_element_type=F32)


def omega(sharers, slot):
    count = sharers[0, slot]
    return jnp.where(count > 0, 1.0 / jnp.maximum(count, 1).astype(F32), 0.0)


def tail_order(count, fold):
    spans = [[k] for k in range(count)]
    while fold and len(spans) > 1:
        half = len(spans) // 2
        spans = [a + b for a, b in zip(spans[:half], spans[half:])]
    return spans[0] if fold else list(range(count))


def pack(out, slot, value, fold):
    count = value.shape[0] // ROWS
    for j in range(count):
        out[slot, j] = value[ROWS * j : ROWS * (j + 1), :LANES].astype(BF16)
    end = value[:, LANES:]
    if fold:
        while end.shape[0] > ROWS:
            half = end.shape[0] // 2
            end = jnp.concatenate([end[:half], end[half:]], axis=1)
    else:
        end = jnp.concatenate([end[ROWS * j : ROWS * (j + 1)] for j in range(count)], axis=1)
    out[slot, count] = end.astype(BF16)


def unpack(ref, slot, rhs, tail, fold):
    count = rhs // ROWS
    main = [ref[slot, j].astype(F32) for j in range(count)]
    last = ref[slot, count].astype(F32)
    order = tail_order(count, fold)
    end = []
    for k in range(count):
        at = order.index(k) * tail
        end.append(last[:, at : at + tail])
    return jnp.concatenate([jnp.concatenate(main, axis=0), jnp.concatenate(end, axis=0)], axis=1)


def loop(count, step, group=16):
    group = min(group, count)

    def body(g, carry):
        for u in range(group):
            step(g * group + u)
        return carry

    lax.fori_loop(0, count // group, body, 0)


def table_loop(table, step):
    rows, group = table.shape

    def body(g, carry):
        row = table[pl.ds(g, 1), :]
        for u in range(group):
            step(g * group + u, row[0, u])
        return carry

    lax.fori_loop(0, rows, body, 0)


def weights(sharers, g):
    count = sharers[pl.ds(g, 1), :]
    return jnp.where(count > 0, 1.0 / jnp.maximum(count, 1).astype(F32), 0.0)


def condense_kernel(
    elem_in, sharers_in, map_in, inner, inv, couple, face, out, elem, sharers, cmap, rin, invs, cps, fac, sems, small
):
    slots, rhs, width = fac.shape
    step = min(slots, CHUNK)
    chunks = slots // step
    copy = pltpu.make_async_copy

    def part(c):
        return pl.ds(c * step, step)

    def couple_copy(c):
        return copy(couple.at[part(c)], cps.at[part(c)], sems.at[2, c])

    def face_copy(c):
        return copy(face.at[part(c)], fac.at[part(c)], sems.at[3, c])

    first = copy(elem_in, elem, small.at[0])
    others = [copy(sharers_in, sharers, small.at[1]), copy(map_in, cmap, small.at[2])]
    first.start()
    for other in others:
        other.start()
    couple_copy(0).start()
    face_copy(0).start()
    first.wait()
    for c in range(chunks):
        for u in range(step):
            l = c * step + u
            copy(inner.at[elem[0, l]], rin.at[l], sems.at[0, c]).start()
            copy(inv.at[elem[0, l]], invs.at[l], sems.at[1, c]).start()
        if c > 0:
            couple_copy(c).start()
            face_copy(c).start()
    for other in others:
        other.wait()
    maps = cmap[...]
    digits = jnp.concatenate([maps // DIGIT, maps % DIGIT], axis=0).astype(F32)
    local = digits.shape[1]
    digits = jnp.concatenate([jnp.zeros((ROWS, LANES - local), F32), digits], axis=1).astype(BF16)
    last = out.shape[1] - 1
    for c in range(chunks):
        copy(inner.at[pl.ds(0, step)], rin.at[part(c)], sems.at[0, c]).wait()
        copy(inv.at[pl.ds(0, step)], invs.at[part(c)], sems.at[1, c]).wait()
        near = [dot(rin[c * step + u], invs[c * step + u], NT).astype(BF16) for u in range(step)]
        couple_copy(c).wait()
        face_copy(c).wait()
        for u in range(step):
            l = c * step + u
            value = fac[l].astype(F32) - dot(near[u], cps[l], NT)
            pack(out, l, omega(sharers, l) * value, False)
            out[l, last] = digits


def assemble(recv, got, out, sums, rounded):
    rows = sums.shape[1]
    owned = sums.shape[0] - 1
    sums[...] = jnp.zeros_like(sums)

    def add(s, j):
        sums[j] += got[s, :rows].astype(F32)

    table_loop(recv, add)
    rounded[...] = sums[...].astype(BF16)
    rounded[owned] = jnp.zeros(rounded.shape[1:], BF16)

    def give(s, j):
        out[s, :rows] = rounded[j]

    table_loop(recv, give)


def pair_digits(first, d, local):
    last = first.shape[1] - 1
    at = LANES - local
    low = first[d, last].astype(F32)
    top = first[d + 1, last].astype(F32)
    both = jnp.concatenate([low[:2, at:], top[:2, at:]], axis=1).astype(jnp.int32)
    return both[0:1], both[1:2]


def take_lanes(ref, tile, lane):
    rows, total = ref.shape
    lane = jnp.broadcast_to(lane, (rows, LANES))
    tile = jnp.broadcast_to(tile, (rows, LANES))
    taken = None
    for t in range(total // LANES):
        part = jnp.take_along_axis(ref[:, t * LANES : (t + 1) * LANES], lane, axis=1)
        taken = part if taken is None else jnp.where(tile == t, part, taken)
    return taken


def owner_kernel(recv, got, out, sums, rounded):
    assemble(recv, got, out, sums, rounded)


def halves(value, local, left):
    half = value.shape[0] // 2
    top, low = value[:half], value[half:]
    return jnp.where(left, top, pltpu.roll(low, local, 1)), jnp.where(left, pltpu.roll(top, local, 1), low)


def first_owner_kernel(recv, got, cinv, out, sums, rounded, strip):
    slots, height, _, _ = out.shape
    head = sums.shape[1]
    piece = strip.shape[0]
    local = LANES // 2
    start = pl.multiple_of(lax.axis_index("sub") * piece, piece)
    strip[...] = cinv[pl.ds(start, piece), :]
    left = lax.broadcasted_iota(jnp.int32, (piece // 2, LANES), 1) < local

    def step(p):
        taken = take_lanes(strip, *pair_digits(got, 2 * p, local))
        low, top = halves(taken, local, left)
        for j in range(height - head):
            out[2 * p, head + j] = low[ROWS * j : ROWS * (j + 1)].astype(BF16)
            out[2 * p + 1, head + j] = top[ROWS * j : ROWS * (j + 1)].astype(BF16)

    loop(slots // 2, step)
    assemble(recv, got, out, sums, rounded)


def restrict_kernel(sharers, got, basis, out, restricted, total):
    slots, rhs, width = restricted.shape
    tail = width - LANES
    groups, group = sharers.shape
    total[...] = jnp.zeros_like(total)

    def body(g, carry):
        part = None
        weight = weights(sharers, g)
        for u in range(group):
            l = g * group + u
            value = (weight[:, u : u + 1] * unpack(got, l, rhs, tail, False)).astype(BF16)
            restricted[l] = value
            term = dot(value, basis[l], NT)
            part = term if part is None else part + term
        total[...] += part
        return carry

    lax.fori_loop(0, groups, body, 0)
    both = total[...]
    block = jnp.concatenate([both[: rhs // 2], both[rhs // 2 :]], axis=1).astype(BF16)

    def give(d):
        out[d] = block

    loop(slots, give, 32)


def turn_columns(groups, rows, got, head, turned):
    local, total = turned.shape
    piece = (got.shape[1] - head) * ROWS * 2
    for t in range(total // LANES):
        parts = []
        for k in range(t * LANES, (t + 1) * LANES, piece):
            device = (k % rows) // piece * groups + k // rows
            block = [got[device, j].astype(F32) for j in range(head, got.shape[1])]
            block = jnp.concatenate(block, axis=0)
            parts += [block, pltpu.roll(block, local, 1)]
        turned[:, t * LANES : (t + 1) * LANES] = jnp.concatenate(parts, axis=0).T[:local]


def correct_kernel(groups, rows, sharers, got, first, second, restricted, inv, basis, out, turned, sums, near):
    slots, rhs, width = restricted.shape
    head = first.shape[1] - 1
    local = basis.shape[1]
    turn_columns(groups, rows, second, head, turned)
    sums[...] = jnp.zeros_like(sums)
    left = lax.broadcasted_iota(jnp.int32, (rhs // 2, LANES), 1) < local
    group = min(slots // 2, 16)

    def body(g, carry):
        part = None
        for u in range(group):
            p = g * group + u
            columns = take_lanes(turned, *pair_digits(first, 2 * p, local)).astype(BF16)
            low = got[2 * p].astype(F32)
            top = got[2 * p + 1].astype(F32)
            value = jnp.concatenate(halves(jnp.concatenate([low, top], axis=0), local, left), axis=0)
            term = dot(value.astype(BF16), columns, NT)
            part = term if part is None else part + term
            for l in (2 * p, 2 * p + 1):
                near[l] = dot(restricted[l], inv[l], NT)
        sums[...] += part
        return carry

    lax.fori_loop(0, slots // 2 // group, body, 0)
    picked = sums[...].astype(BF16)
    def finish(g, carry):
        weight = weights(sharers, g)
        for u in range(sharers.shape[1]):
            l = g * sharers.shape[1] + u
            value = dot(picked, basis[l]) + near[l]
            pack(out, l, weight[:, u : u + 1] * value, True)
        return carry

    lax.fori_loop(0, sharers.shape[0], finish, 0)


def extend_kernel(elem, got, inner, couple, inv, inner_out, face_out, sums, faces, inners, sems):
    slots, rhs, width = faces.shape
    elements = inners.shape[0]
    tail = width - LANES
    sums[...] = inner[...].astype(F32)

    def step(l, e):
        value = unpack(got, l, rhs, tail, True).astype(BF16)
        faces[l] = value
        sums[e] -= dot(value, couple[l])

    table_loop(elem, step)
    copies = [pltpu.make_async_copy(faces, face_out, sems.at[0])]
    copies[0].start()
    part = elements // 2
    for c in range(2):

        def finish(e):
            inners[c * part + e] = dot(sums[c * part + e].astype(BF16), inv[c * part + e], NT).astype(BF16)

        loop(part, finish, 32)
        span = pl.ds(c * part, part)
        copies.append(pltpu.make_async_copy(inners.at[span], inner_out.at[span], sems.at[1 + c]))
        copies[-1].start()
    for each in copies:
        each.wait()


def padded(shape, dtype):
    size = jnp.dtype(dtype).itemsize
    for n in shape[:-2]:
        size *= n
    high = shape[-2] if shape[-2] < 8 else -(-shape[-2] // 16) * 16
    return size * high * (-(-shape[-1] // LANES) * LANES)


def call(kernel, out_shape, specs, args, scratch=(), flops=0, name=None, limit=None, out_spec=VMEM):
    many = isinstance(out_shape, (tuple, list))
    outs = tuple(out_shape) if many else (out_shape,)
    held = [a for a, s in zip(args, specs) if s is VMEM] + list(outs)
    need = sum(padded(a.shape, a.dtype) for a in held)
    room = sum(padded(shape, dtype) for shape, dtype in scratch if dtype is not None)
    made = [pltpu.VMEM(shape, dtype) if dtype is not None else shape for shape, dtype in scratch]
    return pl.pallas_call(
        kernel,
        out_shape=out_shape,
        in_specs=specs,
        out_specs=tuple(out_spec for _ in outs) if many else out_spec,
        scratch_shapes=made,
        cost_estimate=pl.CostEstimate(flops=flops, bytes_accessed=need, transcendentals=0),
        compiler_params=pltpu.CompilerParams(vmem_limit_bytes=limit or need + room + (2 << 20)),
        name=name,
    )(*args)


def body(
    res_inner,
    res_face,
    inner_inv,
    face_coupling,
    face_elem,
    face_inv,
    coarse_basis,
    coarse_map,
    coarse_inv,
    recv_index,
    sharers,
):
    slots, rhs, width = res_face.shape
    owned = slots // 4
    elements = res_inner.shape[0]
    rows, total = coarse_inv.shape
    local = coarse_map.shape[1]
    groups = total // rows
    piece = rows * groups // slots
    shape = jax.ShapeDtypeStruct
    head = rhs // ROWS + 1
    wire = shape((slots, head, ROWS, LANES), BF16)
    unit = 2 * rhs * width * width
    recv_table, sharers_table, elem_table = (
        x.reshape(-1, min(slots, GROUP)) for x in (recv_index, sharers, face_elem)
    )
    tables = [((owned + 1, head, ROWS, LANES), F32), ((owned + 1, head, ROWS, LANES), BF16)]

    sent = call(
        condense_kernel,
        shape((slots, head + 1, ROWS, LANES), BF16),
        [HBM] * 7,
        tuple(
            pltpu.with_memory_space_constraint(x, pltpu.HBM)
            for x in (face_elem, sharers, coarse_map, res_inner, inner_inv, face_coupling, res_face)
        ),
        [
            (pltpu.SMEM(face_elem.shape, jnp.int32), None),
            (pltpu.SMEM(sharers.shape, jnp.int32), None),
            (pltpu.VMEM(coarse_map.shape, jnp.int32), None),
            ((slots, rhs, width), BF16),
            ((slots, width, width), BF16),
            ((slots, width, width), BF16),
            ((slots, rhs, width), BF16),
            (pltpu.SemaphoreType.DMA((4, -(-slots // CHUNK))), None),
            (pltpu.SemaphoreType.DMA((3,)), None),
        ],
        flops=2 * slots * unit,
        name="condense",
    )
    first = exchange(sent)
    held = call(
        first_owner_kernel,
        shape((slots, head + piece // (2 * ROWS), ROWS, LANES), BF16),
        [VMEM, VMEM, VMEM],
        (recv_table, first, coarse_inv),
        tables + [((piece, total), F32)],
        flops=100 * slots * unit,
        name="first_owner",
    )
    gathered = exchange(held)
    coarse, restricted = call(
        restrict_kernel,
        (shape((slots, rhs // 2, LANES), BF16), shape((slots, rhs, width), BF16)),
        [VMEM, VMEM, VMEM],
        (sharers_table, gathered, coarse_basis),
        [((rhs, local), F32)],
        flops=100 * slots * unit,
        name="restrict",
    )
    every = exchange(coarse)
    weighted = call(
        functools.partial(correct_kernel, groups, rows),
        wire,
        [VMEM] * 7,
        (sharers_table, every, first, gathered, restricted, face_inv, coarse_basis),
        [((local, total), F32), ((rhs, local), F32), ((slots, rhs, width), F32)],
        flops=2 * slots * unit,
        name="correct",
    )
    third = exchange(weighted)
    spread = call(
        owner_kernel, wire, [VMEM, VMEM], (recv_table, third), tables, flops=slots * width * LANES, name="owner"
    )
    assembled = exchange(spread)
    return call(
        extend_kernel,
        (shape((elements, rhs, width), BF16), shape((slots, rhs, width), BF16)),
        [VMEM] * 5,
        (elem_table, assembled, res_inner, face_coupling, inner_inv),
        [
            ((elements, rhs, width), F32),
            ((slots, rhs, width), BF16),
            ((elements, rhs, width), BF16),
            (pltpu.SemaphoreType.DMA((3,)), None),
        ],
        flops=2 * slots * unit,
        name="extend",
        out_spec=HBM,
    )


def solution(mesh):
    block = P(AXES, None, None)
    row = P(AXES, None)
    return jax.shard_map(
        body,
        mesh=mesh,
        in_specs=(block, block, block, block, row, block, block, row, P("grp", None), row, row),
        out_specs=(block, block),
        check_vma=False,
    )
```

```python
import functools

import jax
import jax.numpy as jnp
from jax import lax
from jax.experimental import pallas as pl
from jax.experimental.pallas import tpu as pltpu
from jax.sharding import PartitionSpec as P

AXES = ("sub", "grp")
DIGIT = 128
LANES = 128
NT = (((1,), (1,)), ((), ()))
NN = (((1,), (0,)), ((), ()))
F32 = jnp.float32
BF16 = jnp.bfloat16
VMEM = pl.BlockSpec(memory_space=pltpu.VMEM)
HBM = pl.BlockSpec(memory_space=pltpu.HBM)
CHUNK = 16
ROWS = 2
GROUP = 32


def exchange(blocks):
    return lax.all_to_all(blocks, AXES, split_axis=0, concat_axis=0, tiled=True)


def dot(a, b, dims=NN):
    return lax.dot_general(a, b, dims, preferred_element_type=F32)


def omega(sharers, slot):
    count = sharers[0, slot]
    return jnp.where(count > 0, 1.0 / jnp.maximum(count, 1).astype(F32), 0.0)


def tail_order(count, fold):
    spans = [[k] for k in range(count)]
    while fold and len(spans) > 1:
        half = len(spans) // 2
        spans = [a + b for a, b in zip(spans[:half], spans[half:])]
    return spans[0] if fold else list(range(count))


def pack(out, slot, value, fold):
    count = value.shape[0] // ROWS
    for j in range(count):
        out[slot, j] = value[ROWS * j : ROWS * (j + 1), :LANES].astype(BF16)
    end = value[:, LANES:]
    if fold:
        while end.shape[0] > ROWS:
            half = end.shape[0] // 2
            end = jnp.concatenate([end[:half], end[half:]], axis=1)
    else:
        end = jnp.concatenate([end[ROWS * j : ROWS * (j + 1)] for j in range(count)], axis=1)
    out[slot, count] = end.astype(BF16)


def unpack(ref, slot, rhs, tail, fold):
    count = rhs // ROWS
    main = [ref[slot, j].astype(F32) for j in range(count)]
    last = ref[slot, count].astype(F32)
    order = tail_order(count, fold)
    end = []
    for k in range(count):
        at = order.index(k) * tail
        end.append(last[:, at : at + tail])
    return jnp.concatenate([jnp.concatenate(main, axis=0), jnp.concatenate(end, axis=0)], axis=1)


def loop(count, step, group=16):
    group = min(group, count)

    def body(g, carry):
        for u in range(group):
            step(g * group + u)
        return carry

    lax.fori_loop(0, count // group, body, 0)


def table_loop(table, step):
    rows, group = table.shape

    def body(g, carry):
        row = table[pl.ds(g, 1), :]
        for u in range(group):
            step(g * group + u, row[0, u])
        return carry

    lax.fori_loop(0, rows, body, 0)


def weights(sharers, g):
    count = sharers[pl.ds(g, 1), :]
    return jnp.where(count > 0, 1.0 / jnp.maximum(count, 1).astype(F32), 0.0)


def condense_kernel(
    elem_in, sharers_in, map_in, inner, inv, couple, face, out, elem, sharers, cmap, rin, invs, cps, fac, sems, small
):
    slots, rhs, width = fac.shape
    step = min(slots, CHUNK)
    chunks = slots // step
    copy = pltpu.make_async_copy

    def part(c):
        return pl.ds(c * step, step)

    def couple_copy(c):
        return copy(couple.at[part(c)], cps.at[part(c)], sems.at[2, c])

    def face_copy(c):
        return copy(face.at[part(c)], fac.at[part(c)], sems.at[3, c])

    first = copy(elem_in, elem, small.at[0])
    others = [copy(sharers_in, sharers, small.at[1]), copy(map_in, cmap, small.at[2])]
    first.start()
    for other in others:
        other.start()
    couple_copy(0).start()
    face_copy(0).start()
    first.wait()
    for c in range(chunks):
        for u in range(step):
            l = c * step + u
            copy(inner.at[elem[0, l]], rin.at[l], sems.at[0, c]).start()
            copy(inv.at[elem[0, l]], invs.at[l], sems.at[1, c]).start()
        if c > 0:
            couple_copy(c).start()
            face_copy(c).start()
    for other in others:
        other.wait()
    maps = cmap[...]
    digits = jnp.concatenate([maps // DIGIT, maps % DIGIT], axis=0).astype(F32)
    local = digits.shape[1]
    digits = jnp.concatenate([jnp.zeros((ROWS, LANES - local), F32), digits], axis=1).astype(BF16)
    last = out.shape[1] - 1
    for c in range(chunks):
        copy(inner.at[pl.ds(0, step)], rin.at[part(c)], sems.at[0, c]).wait()
        copy(inv.at[pl.ds(0, step)], invs.at[part(c)], sems.at[1, c]).wait()
        near = [dot(rin[c * step + u], invs[c * step + u], NT).astype(BF16) for u in range(step)]
        couple_copy(c).wait()
        face_copy(c).wait()
        for u in range(step):
            l = c * step + u
            value = fac[l].astype(F32) - dot(near[u], cps[l], NT)
            pack(out, l, omega(sharers, l) * value, False)
            out[l, last] = digits


def assemble(recv, got, out, sums, rounded):
    rows = sums.shape[1]
    owned = sums.shape[0] - 1
    sums[...] = jnp.zeros_like(sums)

    def add(s, j):
        sums[j] += got[s, :rows].astype(F32)

    table_loop(recv, add)
    rounded[...] = sums[...].astype(BF16)
    rounded[owned] = jnp.zeros(rounded.shape[1:], BF16)

    def give(s, j):
        out[s, :rows] = rounded[j]

    table_loop(recv, give)


def pair_digits(first, d, local):
    last = first.shape[1] - 1
    at = LANES - local
    low = first[d, last].astype(F32)
    top = first[d + 1, last].astype(F32)
    both = jnp.concatenate([low[:2, at:], top[:2, at:]], axis=1).astype(jnp.int32)
    return both[0:1], both[1:2]


def take_lanes(ref, tile, lane):
    rows, total = ref.shape
    lane = jnp.broadcast_to(lane, (rows, LANES))
    tile = jnp.broadcast_to(tile, (rows, LANES))
    taken = None
    for t in range(total // LANES):
        part = jnp.take_along_axis(ref[:, t * LANES : (t + 1) * LANES], lane, axis=1)
        taken = part if taken is None else jnp.where(tile == t, part, taken)
    return taken


def owner_kernel(recv, got, out, sums, rounded):
    assemble(recv, got, out, sums, rounded)


def halves(value, local, left):
    half = value.shape[0] // 2
    top, low = value[:half], value[half:]
    return jnp.where(left, top, pltpu.roll(low, local, 1)), jnp.where(left, pltpu.roll(top, local, 1), low)


def first_owner_kernel(recv, got, cinv, out, sums, rounded, strip):
    slots, height, _, _ = out.shape
    head = sums.shape[1]
    piece = strip.shape[0]
    local = LANES // 2
    start = pl.multiple_of(lax.axis_index("sub") * piece, piece)
    strip[...] = cinv[pl.ds(start, piece), :]
    left = lax.broadcasted_iota(jnp.int32, (piece // 2, LANES), 1) < local

    def step(p):
        taken = take_lanes(strip, *pair_digits(got, 2 * p, local))
        low, top = halves(taken, local, left)
        for j in range(height - head):
            out[2 * p, head + j] = low[ROWS * j : ROWS * (j + 1)].astype(BF16)
            out[2 * p + 1, head + j] = top[ROWS * j : ROWS * (j + 1)].astype(BF16)

    loop(slots // 2, step)
    assemble(recv, got, out, sums, rounded)


def restrict_kernel(sharers, got, basis, out, restricted, total):
    slots, rhs, width = restricted.shape
    tail = width - LANES
    groups, group = sharers.shape
    total[...] = jnp.zeros_like(total)

    def body(g, carry):
        part = None
        weight = weights(sharers, g)
        for u in range(group):
            l = g * group + u
            value = (weight[:, u : u + 1] * unpack(got, l, rhs, tail, False)).astype(BF16)
            restricted[l] = value
            term = dot(value, basis[l], NT)
            part = term if part is None else part + term
        total[...] += part
        return carry

    lax.fori_loop(0, groups, body, 0)
    both = total[...]
    block = jnp.concatenate([both[: rhs // 2], both[rhs // 2 :]], axis=1).astype(BF16)

    def give(d):
        out[d] = block

    loop(slots, give, 32)


def turn_columns(groups, rows, got, head, turned):
    local, total = turned.shape
    piece = (got.shape[1] - head) * ROWS * 2
    for t in range(total // LANES):
        parts = []
        for k in range(t * LANES, (t + 1) * LANES, piece):
            device = (k % rows) // piece * groups + k // rows
            block = [got[device, j].astype(F32) for j in range(head, got.shape[1])]
            block = jnp.concatenate(block, axis=0)
            parts += [block, pltpu.roll(block, local, 1)]
        turned[:, t * LANES : (t + 1) * LANES] = jnp.concatenate(parts, axis=0).T[:local]


def correct_kernel(groups, rows, sharers, got, first, second, restricted, inv, basis, out, turned, sums, near):
    slots, rhs, width = restricted.shape
    head = first.shape[1] - 1
    local = basis.shape[1]
    turn_columns(groups, rows, second, head, turned)
    sums[...] = jnp.zeros_like(sums)
    left = lax.broadcasted_iota(jnp.int32, (rhs // 2, LANES), 1) < local
    group = min(slots // 2, 16)

    def body(g, carry):
        part = None
        for u in range(group):
            p = g * group + u
            columns = take_lanes(turned, *pair_digits(first, 2 * p, local)).astype(BF16)
            low = got[2 * p].astype(F32)
            top = got[2 * p + 1].astype(F32)
            value = jnp.concatenate(halves(jnp.concatenate([low, top], axis=0), local, left), axis=0)
            term = dot(value.astype(BF16), columns, NT)
            part = term if part is None else part + term
            for l in (2 * p, 2 * p + 1):
                near[l] = dot(restricted[l], inv[l], NT)
        sums[...] += part
        return carry

    lax.fori_loop(0, slots // 2 // group, body, 0)
    picked = sums[...].astype(BF16)
    def finish(g, carry):
        weight = weights(sharers, g)
        for u in range(sharers.shape[1]):
            l = g * sharers.shape[1] + u
            value = dot(picked, basis[l]) + near[l]
            pack(out, l, weight[:, u : u + 1] * value, True)
        return carry

    lax.fori_loop(0, sharers.shape[0], finish, 0)


def extend_kernel(elem, got, inner, couple, inv, inner_out, face_out, sums, faces, inners, sems):
    slots, rhs, width = faces.shape
    elements = inners.shape[0]
    tail = width - LANES
    sums[...] = inner[...].astype(F32)

    def step(l, e):
        value = unpack(got, l, rhs, tail, True).astype(BF16)
        faces[l] = value
        sums[e] -= dot(value, couple[l])

    table_loop(elem, step)
    copies = [pltpu.make_async_copy(faces, face_out, sems.at[0])]
    copies[0].start()
    parts = sems.shape[0] - 1
    part = elements // parts
    for c in range(parts):

        def finish(e):
            inners[c * part + e] = dot(sums[c * part + e].astype(BF16), inv[c * part + e], NT).astype(BF16)

        loop(part, finish, 32)
        span = pl.ds(c * part, part)
        copies.append(pltpu.make_async_copy(inners.at[span], inner_out.at[span], sems.at[1 + c]))
        copies[-1].start()
    for each in copies:
        each.wait()


def padded(shape, dtype):
    size = jnp.dtype(dtype).itemsize
    for n in shape[:-2]:
        size *= n
    high = shape[-2] if shape[-2] < 8 else -(-shape[-2] // 16) * 16
    return size * high * (-(-shape[-1] // LANES) * LANES)


def call(kernel, out_shape, specs, args, scratch=(), flops=0, name=None, limit=None, out_spec=VMEM):
    many = isinstance(out_shape, (tuple, list))
    outs = tuple(out_shape) if many else (out_shape,)
    held = [a for a, s in zip(args, specs) if s is VMEM] + list(outs)
    need = sum(padded(a.shape, a.dtype) for a in held)
    room = sum(padded(shape, dtype) for shape, dtype in scratch if dtype is not None)
    made = [pltpu.VMEM(shape, dtype) if dtype is not None else shape for shape, dtype in scratch]
    return pl.pallas_call(
        kernel,
        out_shape=out_shape,
        in_specs=specs,
        out_specs=tuple(out_spec for _ in outs) if many else out_spec,
        scratch_shapes=made,
        cost_estimate=pl.CostEstimate(flops=flops, bytes_accessed=need, transcendentals=0),
        compiler_params=pltpu.CompilerParams(vmem_limit_bytes=limit or need + room + (2 << 20)),
        name=name,
    )(*args)


def body(
    res_inner,
    res_face,
    inner_inv,
    face_coupling,
    face_elem,
    face_inv,
    coarse_basis,
    coarse_map,
    coarse_inv,
    recv_index,
    sharers,
):
    slots, rhs, width = res_face.shape
    owned = slots // 4
    elements = res_inner.shape[0]
    rows, total = coarse_inv.shape
    local = coarse_map.shape[1]
    groups = total // rows
    piece = rows * groups // slots
    shape = jax.ShapeDtypeStruct
    head = rhs // ROWS + 1
    wire = shape((slots, head, ROWS, LANES), BF16)
    unit = 2 * rhs * width * width
    recv_table, sharers_table, elem_table = (
        x.reshape(-1, min(slots, GROUP)) for x in (recv_index, sharers, face_elem)
    )
    tables = [((owned + 1, head, ROWS, LANES), F32), ((owned + 1, head, ROWS, LANES), BF16)]

    sent = call(
        condense_kernel,
        shape((slots, head + 1, ROWS, LANES), BF16),
        [HBM] * 7,
        tuple(
            pltpu.with_memory_space_constraint(x, pltpu.HBM)
            for x in (face_elem, sharers, coarse_map, res_inner, inner_inv, face_coupling, res_face)
        ),
        [
            (pltpu.SMEM(face_elem.shape, jnp.int32), None),
            (pltpu.SMEM(sharers.shape, jnp.int32), None),
            (pltpu.VMEM(coarse_map.shape, jnp.int32), None),
            ((slots, rhs, width), BF16),
            ((slots, width, width), BF16),
            ((slots, width, width), BF16),
            ((slots, rhs, width), BF16),
            (pltpu.SemaphoreType.DMA((4, -(-slots // CHUNK))), None),
            (pltpu.SemaphoreType.DMA((3,)), None),
        ],
        flops=2 * slots * unit,
        name="condense",
    )
    first = exchange(sent)
    held = call(
        first_owner_kernel,
        shape((slots, head + piece // (2 * ROWS), ROWS, LANES), BF16),
        [VMEM, VMEM, VMEM],
        (recv_table, first, coarse_inv),
        tables + [((piece, total), F32)],
        flops=100 * slots * unit,
        name="first_owner",
    )
    gathered = exchange(held)
    coarse, restricted = call(
        restrict_kernel,
        (shape((slots, rhs // 2, LANES), BF16), shape((slots, rhs, width), BF16)),
        [VMEM, VMEM, VMEM],
        (sharers_table, gathered, coarse_basis),
        [((rhs, local), F32)],
        flops=100 * slots * unit,
        name="restrict",
    )
    every = exchange(coarse)
    weighted = call(
        functools.partial(correct_kernel, groups, rows),
        wire,
        [VMEM] * 7,
        (sharers_table, every, first, gathered, restricted, face_inv, coarse_basis),
        [((local, total), F32), ((rhs, local), F32), ((slots, rhs, width), F32)],
        flops=2 * slots * unit,
        name="correct",
    )
    third = exchange(weighted)
    spread = call(
        owner_kernel, wire, [VMEM, VMEM], (recv_table, third), tables, flops=slots * width * LANES, name="owner"
    )
    assembled = exchange(spread)
    return call(
        extend_kernel,
        (shape((elements, rhs, width), BF16), shape((slots, rhs, width), BF16)),
        [VMEM] * 5,
        (elem_table, assembled, res_inner, face_coupling, inner_inv),
        [
            ((elements, rhs, width), F32),
            ((slots, rhs, width), BF16),
            ((elements, rhs, width), BF16),
            (pltpu.SemaphoreType.DMA((5,)), None),
        ],
        flops=2 * slots * unit,
        name="extend",
        out_spec=HBM,
    )


def solution(mesh):
    block = P(AXES, None, None)
    row = P(AXES, None)
    return jax.shard_map(
        body,
        mesh=mesh,
        in_specs=(block, block, block, block, row, block, block, row, P("grp", None), row, row),
        out_specs=(block, block),
        check_vma=False,
    )
```
